32 devices in a mesh: dp: 8 (over y, x, core), mp: 4 (over z).
Axes of the slice: x: 2, y: 2, z: 4, core: 2. Of those that a mesh axis runs over, the one named last changes fastest.
Arguments:
- tokens_in: bfloat16 [16384, 640], P(('dp', 'mp')), may hold values from -6 to 6
- cotangent: bfloat16 [16384, 640], P(('dp', 'mp')), may hold values from -6 to 6
- lengths: int32 [8, 32], P('dp'), may hold values from 0 to 1024, as said below
- segments: int32 [8, 2048], P('dp'), may hold values from 0 to 32, as said below
- bucket_map: int32 [8], P('dp'), may hold values from 0 to 3, as said below
- bucket_tokens: int32 [4], replicated, may hold values from 256 to 65535
- attention: float32 [2, 4, 640, 640], P(None, None, 'dp', 'mp')
- feedforward: float32 [2, 2, 640, 5120], P(None, None, 'dp', 'mp')
- vectors: float32 [2, 6, 640], P(None, None, 'dp')
- head_bias: float32 [2, 2, 640], P(None, None, 'mp'), may hold values from -3 to 3
- unit_bias: float32 [2, 5120], P(None, 'mp'), may hold values from -3 to 3
- attention_moment: float32 [2, 4, 640, 640], P(None, None, 'dp', 'mp'), may hold values from -384 to 384
- feedforward_moment: float32 [2, 2, 640, 5120], P(None, None, 'dp', 'mp'), may hold values from -384 to 384
- vectors_moment: float32 [2, 6, 640], P(None, None, 'dp'), may hold values from -384 to 384
- head_moment: float32 [2, 2, 640], P(None, None, 'mp'), may hold values from -384 to 384
- unit_moment: float32 [2, 5120], P(None, 'mp'), may hold values from -384 to 384
- attention_mean: float32 [2, 4, 640, 640], P(None, None, 'dp', 'mp')
- feedforward_mean: float32 [2, 2, 640, 5120], P(None, None, 'dp', 'mp')
- vectors_mean: float32 [2, 6, 640], P(None, None, 'dp')
- head_mean: float32 [2, 2, 640], P(None, None, 'mp'), may hold values from -3 to 3
- unit_mean: float32 [2, 5120], P(None, 'mp'), may hold values from -3 to 3
Outputs:
- hidden_out: float32 [16384, 640], P(('dp', 'mp'))
- input_gradient: float32 [16384, 640], P(('dp', 'mp'))
- attention_gradient: float32 [2, 4, 640, 640], P(None, None, 'dp', 'mp')
- feedforward_gradient: float32 [2, 2, 640, 5120], P(None, None, 'dp', 'mp')
- vectors_gradient: float32 [2, 6, 640], P(None, None, 'dp')
- head_gradient: float32 [2, 2, 640], P(None, None, 'mp')
- unit_gradient: float32 [2, 5120], P(None, 'mp')
- attention_next: float32 [2, 4, 640, 640], P(None, None, 'dp', 'mp')
- feedforward_next: float32 [2, 2, 640, 5120], P(None, None, 'dp', 'mp')
- vectors_next: float32 [2, 6, 640], P(None, None, 'dp')
- head_next: float32 [2, 2, 640], P(None, None, 'mp')
- unit_next: float32 [2, 5120], P(None, 'mp')
- attention_momentum: float32 [2, 4, 640, 640], P(None, None, 'dp', 'mp')
- feedforward_momentum: float32 [2, 2, 640, 5120], P(None, None, 'dp', 'mp')
- vectors_momentum: float32 [2, 6, 640], P(None, None, 'dp')
- head_momentum: float32 [2, 2, 640], P(None, None, 'mp')
- unit_momentum: float32 [2, 5120], P(None, 'mp')
- attention_average: float32 [2, 4, 640, 640], P(None, None, 'dp', 'mp')
- feedforward_average: float32 [2, 2, 640, 5120], P(None, None, 'dp', 'mp')
- vectors_average: float32 [2, 6, 640], P(None, None, 'dp')
- head_average: float32 [2, 2, 640], P(None, None, 'mp')
- unit_average: float32 [2, 5120], P(None, 'mp')
- attention_copy: bfloat16 [2, 4, 640, 640], P(None, None, 'dp', 'mp')
- feedforward_copy: bfloat16 [2, 2, 640, 5120], P(None, None, 'dp', 'mp')
The draws below stay inside these ranges and needn't reach their ends.
Inputs may be any that keep to these rules, and one draw needn't show every extreme that they name: In each pack the nonzero lengths stand first and are 20 or more; a pack's lengths sum to less than 2048; some pack holds a sequence of 1024. segments[p, t] is the number of sequences of pack p that end at or before position t, so positions past the sum of the pack's lengths hold 32. `bucket_map`: each bucket owns a run of 2 consecutive packs.
All inputs are finite; a program needn't handle non-finite values.
Results may differ from the reference program's by a relative error of at most 0.012.
Values may be sent and summed in bfloat16 or wider, within the bound.
A program may use at most 256 MiB of HBM per device.

```python
import jax
import jax.numpy as jnp
from jax import lax

D = 640
HEADS = 20
HEAD_DIM = 32
FF = 5120
LAYERS = 2
TOK_DEV = 2048
MAX_LEN = 1024
MIN_LEN = 20
SLOTS = 32
BUCKETS = 4
PACKS = 8
TOKENS = 16384


def slot_normal(key, shape, slot_scales):
    values = jax.random.truncated_normal(key, -4.0, 4.0, shape, jnp.float32)
    factors = jnp.asarray(slot_scales, jnp.float32).reshape((1, len(slot_scales)) + (1,) * (len(shape) - 2))
    return values * factors


def attention_slots(key):
    fan_scale = D ** (-0.5)
    return slot_normal(key, (LAYERS, 4, D, D), [fan_scale, fan_scale, fan_scale, (D // 32) ** (-0.5)])


def feedforward_slots(key):
    return slot_normal(key, (LAYERS, 2, D, FF), [D ** (-0.5), FF ** (-0.5)])


def vector_rows(key):
    gain_key, shift_key = jax.random.split(key)
    gains = 1.0 + 0.3 * jax.random.uniform(gain_key, (LAYERS, 6, D), jnp.float32, -1.0, 1.0)
    shifts = 0.3 * jax.random.truncated_normal(shift_key, -3.0, 3.0, (LAYERS, 6, D), jnp.float32)
    row_index = jnp.arange(6)
    is_gain = (row_index % 2 == 0) & (row_index < 4)
    return jnp.where(is_gain[None, :, None], gains, shifts)


def draw_attention(key, part):
    return attention_slots(jax.random.fold_in(key, 1))


def draw_attention_mean(key, part):
    return attention_slots(jax.random.fold_in(key, 2))


def draw_feedforward(key, part):
    return feedforward_slots(jax.random.fold_in(key, 3))


def draw_feedforward_mean(key, part):
    return feedforward_slots(jax.random.fold_in(key, 4))


def draw_vectors(key, part):
    return vector_rows(jax.random.fold_in(key, 5))


def draw_vectors_mean(key, part):
    return vector_rows(jax.random.fold_in(key, 6))


def pack_layout(key):
    base_key = jax.random.fold_in(key, 11)
    order_key, length_key, spare_key = jax.random.split(base_key, 3)
    bucket_order = jax.random.permutation(order_key, BUCKETS).astype(jnp.int32)
    devices = jnp.arange(PACKS, dtype=jnp.int32)
    bucket = bucket_order[devices * BUCKETS // PACKS].astype(jnp.int32)
    ceiling = MIN_LEN + (bucket + 1) * (bucket + 1) * (MAX_LEN - MIN_LEN) // (BUCKETS * BUCKETS)
    drawn_lengths = jax.random.randint(length_key, (PACKS, SLOTS), MIN_LEN, ceiling[:, None] + 1, dtype=jnp.int32)
    target = jnp.argmax((bucket == BUCKETS - 1).astype(jnp.int32)).astype(jnp.int32)
    slot_index = jnp.arange(SLOTS, dtype=jnp.int32)
    drawn_lengths = jnp.where((devices[:, None] == target) & (slot_index[None, :] == 0), MAX_LEN, drawn_lengths).astype(jnp.int32)
    spare_room = jax.random.randint(spare_key, (PACKS, 1), 1, 4 * MIN_LEN + 1, dtype=jnp.int32)
    running_end = jnp.cumsum(drawn_lengths, axis=1)
    kept_lengths = jnp.where(running_end <= TOK_DEV - spare_room, drawn_lengths, 0).astype(jnp.int32)
    finish = jnp.cumsum(kept_lengths, axis=1)
    places = jnp.arange(TOK_DEV, dtype=jnp.int32)
    segment_ids = jnp.sum((finish[:, None, :] <= places[None, :, None]).astype(jnp.int32), axis=2).astype(jnp.int32)
    return (kept_lengths, segment_ids, bucket)


def draw_lengths(key, part):
    return pack_layout(key)[0]


def draw_segments(key, part):
    return pack_layout(key)[1]


def draw_bucket_map(key, part):
    return pack_layout(key)[2]


def set_ends(values, rng, least, high):
    extent = values.shape
    spot = [jax.random.randint(jax.random.fold_in(rng, axis), (), 0, extent[axis]) for axis in range(len(extent))]
    values = values.at[tuple(spot)].set(least)
    longest = extent.index(max(extent))
    spot[longest] = (spot[longest] + 1) % extent[longest]
    return values.at[tuple(spot)].set(high)


def levels(own_key, extent, shards, smallest, largest):
    def one(position, parts):
        draws = jax.random.uniform(jax.random.fold_in(jax.random.fold_in(own_key, 6), position), (parts,), jnp.float32, smallest / len(shards), largest / len(shards))
        return jnp.repeat(jnp.exp(draws), extent[position] // parts).reshape((-1,) + (1,) * (len(extent) - position - 1))

    loudness = one(*shards[0])
    for cut in shards[1:]:
        loudness = loudness * one(*cut)
    return loudness


def bell_draw(key, shape, width, limit, cuts=(), kind=jnp.bfloat16):
    result = jax.random.normal(key, shape, jnp.float32) * width
    if len(cuts) > 0:
        result = levels(key, shape, cuts, -0.22, 0.18) * result
    return jnp.clip(result, min=-limit, max=limit).astype(kind)


def setup_inputs(seed: int = 0) -> dict:
    keys = jax.random.split(jax.random.key(seed), 22)
    tokens_in = bell_draw(keys[0], (TOKENS, D), 1.0, 6.0, ((0, 32),))
    cotangent = bell_draw(keys[1], (TOKENS, D), 1.0, 6.0, ((0, 32),))
    lengths = draw_lengths(jax.random.fold_in(keys[21], 71), 0)
    segments = draw_segments(jax.random.fold_in(keys[21], 71), 0)
    bucket_map = draw_bucket_map(jax.random.fold_in(keys[21], 71), 0)
    bucket_tokens = set_ends(jax.random.randint(keys[5], (BUCKETS,), 256, 65536), jax.random.fold_in(keys[5], 1), 256, 65535).astype(jnp.int32)
    attention = draw_attention(jax.random.fold_in(keys[21], 71), 0)
    feedforward = draw_feedforward(jax.random.fold_in(keys[21], 71), 0)
    vectors = draw_vectors(jax.random.fold_in(keys[21], 71), 0)
    head_bias = bell_draw(keys[9], (LAYERS, 2, D), 0.5, 3.0, ((2, 4),), jnp.float32)
    unit_bias = bell_draw(keys[10], (LAYERS, FF), 0.5, 3.0, ((1, 4),), jnp.float32)
    attention_moment = bell_draw(keys[11], (LAYERS, 4, D, D), (0.5 * TOKENS ** 0.5), 384.0, ((2, 8), (3, 4)), jnp.float32)
    feedforward_moment = bell_draw(keys[12], (LAYERS, 2, D, FF), (0.5 * TOKENS ** 0.5), 384.0, ((2, 8), (3, 4)), jnp.float32)
    vectors_moment = bell_draw(keys[13], (LAYERS, 6, D), (0.5 * TOKENS ** 0.5), 384.0, ((2, 8),), jnp.float32)
    head_moment = bell_draw(keys[14], (LAYERS, 2, D), (0.5 * TOKENS ** 0.5), 384.0, ((2, 4),), jnp.float32)
    unit_moment = bell_draw(keys[15], (LAYERS, FF), (0.5 * TOKENS ** 0.5), 384.0, ((1, 4),), jnp.float32)
    attention_mean = draw_attention_mean(jax.random.fold_in(keys[21], 71), 0)
    feedforward_mean = draw_feedforward_mean(jax.random.fold_in(keys[21], 71), 0)
    vectors_mean = draw_vectors_mean(jax.random.fold_in(keys[21], 71), 0)
    head_mean = bell_draw(keys[19], (LAYERS, 2, D), 0.5, 3.0, ((2, 4),), jnp.float32)
    unit_mean = bell_draw(keys[20], (LAYERS, FF), 0.5, 3.0, ((1, 4),), jnp.float32)
    return {"tokens_in": tokens_in, "cotangent": cotangent, "lengths": lengths, "segments": segments, "bucket_map": bucket_map, "bucket_tokens": bucket_tokens, "attention": attention, "feedforward": feedforward, "vectors": vectors, "head_bias": head_bias, "unit_bias": unit_bias, "attention_moment": attention_moment, "feedforward_moment": feedforward_moment, "vectors_moment": vectors_moment, "head_moment": head_moment, "unit_moment": unit_moment, "attention_mean": attention_mean, "feedforward_mean": feedforward_mean, "vectors_mean": vectors_mean, "head_mean": head_mean, "unit_mean": unit_mean}


EPSILON = 1e-05
MOMENTUM = 0.9
AVERAGE_KEEP = 0.9
WEIGHT_DECAY = 0.0001
RATE_SCALE = 0.02
MASKED = -1e+30
HIGHEST = lax.Precision.HIGHEST

@jax.custom_vjp
def low(v):
    return lax.optimization_barrier(v.astype(jnp.bfloat16)).astype(jnp.float32)

@jax.custom_vjp
def low_back(v):
    return v

def low_keep(v):
    return (low(v), None)

def low_pass(kept, grad):
    return (grad,)

def back_keep(v):
    return (v, None)

def back_low(kept, grad):
    return (low(grad),)
low.defvjp(low_keep, low_pass)
low_back.defvjp(back_keep, back_low)

def matmul(left, right):
    return jnp.dot(left, right, precision=HIGHEST)

def layer_norm(hidden, gain_row, shift_row):
    centre = hidden - lax.optimization_barrier(jnp.mean(hidden, axis=-1, keepdims=True))
    inverse = lax.rsqrt(lax.optimization_barrier(jnp.mean(centre * centre, axis=-1, keepdims=True)) + EPSILON)
    return centre * inverse * gain_row + shift_row

def attend(queries, keys_all, values, allowed):
    score_scale = HEAD_DIM ** (-0.5)

    def one_head(operands):
        query_head, key_head, value_head = operands
        scores = low_back(jnp.einsum('qd,kd->qk', query_head, key_head, precision=HIGHEST) * score_scale)
        scores = jnp.where(allowed, scores, MASKED)
        probability = jax.nn.softmax(scores, axis=-1)
        return jnp.einsum('qk,kd->qd', low(probability), value_head, precision=HIGHEST)

    def split_heads(matrix):
        return matrix.reshape(matrix.shape[0], HEADS, HEAD_DIM).transpose(1, 0, 2)
    outputs = lax.map(jax.checkpoint(one_head), (split_heads(queries), split_heads(keys_all), split_heads(values)))
    return outputs.transpose(1, 0, 2).reshape(queries.shape[0], HEADS * HEAD_DIM)

def encoder(hidden, params, segment_row, live_row):
    attention = low(params[0])
    feedforward = low(params[1])
    vectors = low(params[2])
    head_bias = low(params[3])
    unit_bias = low(params[4])
    positions = jnp.arange(segment_row.shape[0])
    allowed = (segment_row[:, None] == segment_row[None, :]) & (live_row[None, :] | (positions[:, None] == positions[None, :]))
    for layer_index in range(LAYERS):
        normed = low(layer_norm(hidden, vectors[layer_index, 0], vectors[layer_index, 1]))
        queries = low(low_back(matmul(normed, attention[layer_index, 0]) + head_bias[layer_index, 0]))
        keys_all = low(low_back(matmul(normed, attention[layer_index, 1])))
        values = low(low_back(matmul(normed, attention[layer_index, 2]) + head_bias[layer_index, 1]))
        mixed_rows = low(low_back(attend(queries, keys_all, values, allowed)))
        hidden = hidden + low_back(matmul(mixed_rows, attention[layer_index, 3].T) + vectors[layer_index, 4])
        normed_two = low(layer_norm(hidden, vectors[layer_index, 2], vectors[layer_index, 3]))
        before = low_back(matmul(normed_two, feedforward[layer_index, 0]) + unit_bias[layer_index])
        activated = low(jax.nn.gelu(before, approximate=False))
        hidden = hidden + low_back(matmul(activated, feedforward[layer_index, 1].T) + vectors[layer_index, 5])
    return jnp.where(live_row[:, None], hidden, 0.0)

def sgd_step(weight, gradient, moment, average, step_rate):
    decayed = gradient + WEIGHT_DECAY * weight
    moment_next = MOMENTUM * moment + decayed
    weight_next = weight - step_rate * (decayed + MOMENTUM * moment_next)
    average_next = AVERAGE_KEEP * average + (1.0 - AVERAGE_KEEP) * weight_next
    return (weight_next, moment_next, average_next)

def reference(tokens_in, cotangent, lengths, segments, bucket_map, bucket_tokens, attention, feedforward, vectors, head_bias, unit_bias, attention_moment, feedforward_moment, vectors_moment, head_moment, unit_moment, attention_mean, feedforward_mean, vectors_mean, head_mean, unit_mean):
    params = (attention, feedforward, vectors, head_bias, unit_bias)
    counts_float = bucket_tokens.astype(jnp.float32)
    bucket_weight = BUCKETS * counts_float / jnp.sum(counts_float)
    pack_weight = bucket_weight[bucket_map]
    totals = lax.optimization_barrier(jnp.sum(lengths, axis=1))
    live_mask = jnp.arange(TOK_DEV)[None, :] < totals[:, None]
    hidden_packs = tokens_in.astype(jnp.float32).reshape(PACKS, TOK_DEV, D)
    cotangent_packs = cotangent.astype(jnp.float32).reshape(PACKS, TOK_DEV, D)

    def one_pack(summed, operands):
        hidden, backward, segment_row, live_row, factor = operands
        outputs, pullback = jax.vjp(lambda inner_rows, weights: encoder(inner_rows, weights, segment_row, live_row), hidden, params)
        input_part, weight_parts = pullback(backward * factor)
        return (jax.tree.map(jnp.add, summed, weight_parts), (outputs, input_part))
    zero_tree = jax.tree.map(jnp.zeros_like, params)
    gradients, (outputs, input_parts) = lax.scan(one_pack, zero_tree, (hidden_packs, cotangent_packs, segments, live_mask, pack_weight))
    step_rate = RATE_SCALE * lax.rsqrt(jnp.asarray(TOKENS, jnp.float32))
    moments = (attention_moment, feedforward_moment, vectors_moment, head_moment, unit_moment)
    averages = (attention_mean, feedforward_mean, vectors_mean, head_mean, unit_mean)
    results = [sgd_step(params[index], gradients[index], moments[index], averages[index], step_rate) for index in range(5)]
    return (outputs.reshape(TOKENS, D), input_parts.reshape(TOKENS, D), gradients[0], gradients[1], gradients[2], gradients[3], gradients[4], results[0][0], results[1][0], results[2][0], results[3][0], results[4][0], results[0][1], results[1][1], results[2][1], results[3][1], results[4][1], results[0][2], results[1][2], results[2][2], results[3][2], results[4][2], results[0][0].astype(jnp.bfloat16), results[1][0].astype(jnp.bfloat16))
```

```python
import functools, math
import jax, jax.numpy as jnp
from jax import lax
from jax.experimental import pallas as pl
from jax.experimental.pallas import tpu as pltpu
from jax.sharding import PartitionSpec as P

HEAD_DIM = 32
MASKED = -1e30
LOG2E = math.log2(math.e)
SCORE = HEAD_DIM ** (-0.5)
SCORE2 = SCORE * LOG2E
BLK = 256
BF = jnp.bfloat16
F32 = jnp.float32
VMEM_LIMIT = 60 * 1024 * 1024


def cost(micros):
    return pl.CostEstimate(flops=micros * 1100000000, bytes_accessed=1000000, transcendentals=0)


def dot_nn(a, b):
    return lax.dot_general(a, b, (((1,), (0,)), ((), ())), preferred_element_type=F32)


def dot_nt(a, b):
    return lax.dot_general(a, b, (((1,), (1,)), ((), ())), preferred_element_type=F32)


def load_parts(scal, parts, dest, first, rows, sem, axis):
    copies = []
    for i, part in enumerate(parts):
        start = pl.multiple_of(scal[first + i] * rows, rows)
        at = dest.at[pl.ds(start, rows)] if axis == 0 else dest.at[:, pl.ds(start, rows)]
        copies.append(pltpu.make_async_copy(part, at, sem))
    for copy in copies:
        copy.start()
    return copies


def attn_fwd_kernel(nb, npc, *refs):
    scal = refs[0]
    xparts = refs[1:5]
    wparts = refs[5:5 + npc]
    bias, segk, segq, out, lse = refs[5 + npc:10 + npc]
    xs, ws, ks, qt, vt, acc, scores, sems = refs[10 + npc:]
    heads = ks.shape[0]
    width = heads * HEAD_DIM
    rows = xparts[0].shape[0]
    base = 2 * nb
    wcopies = load_parts(scal, wparts, ws, base + 5, wparts[0].shape[0], sems.at[4], 0)
    xcopies = [load_parts(scal, [p], xs, base + i, rows, sems.at[i], 0)[0] for i, p in enumerate(xparts)]
    for c in wcopies:
        c.wait()
    for i in range(4):
        xcopies[i].wait()
        start = pl.multiple_of(scal[base + i] * rows, rows)
        y = dot_nn(xs[pl.ds(start, rows), :], ws[...])
        qt[:, pl.ds(start, rows)] = (y[:, :width] + bias[0:1, :]).T.astype(BF)
        k = y[:, width:2 * width].astype(BF)
        for h in range(heads):
            ks[h, pl.ds(start, rows), :] = k[:, h * HEAD_DIM:(h + 1) * HEAD_DIM]
        vt[:, pl.ds(start, rows)] = (y[:, 2 * width:] + bias[1:2, :]).T.astype(BF)
    lse[...] = jnp.zeros_like(lse)
    per = rows // BLK

    def fold(z):
        return z.reshape(BLK // 8, 8, BLK)

    def q_block(qb, carry):
        q0 = pl.multiple_of(qb * BLK, BLK)
        acc[...] = jnp.zeros_like(acc)
        sq = segq[:, pl.ds(q0, BLK)]
        first, end = scal[qb], scal[nb + qb]

        def score_block(kb, ms):
            k0 = pl.multiple_of(kb * BLK, BLK)
            mask = segk[pl.ds(k0, BLK), :] == sq
            new = []
            for h in range(heads):
                hs = slice(h * HEAD_DIM, (h + 1) * HEAD_DIM)
                s = dot_nn(ks[h, pl.ds(k0, BLK), :], qt[hs, pl.ds(q0, BLK)])
                s = jnp.where(mask, s, MASKED)
                scores[h, kb] = s
                new.append(jnp.maximum(ms[h], jnp.max(fold(s), axis=0)))
            return tuple(new)

        ms = lax.fori_loop(first, end, score_block, (jnp.full((8, BLK), MASKED, F32),) * heads)
        tops = [jnp.max(m, axis=0, keepdims=True) * SCORE2 for m in ms]

        def mix_block(kb, ls):
            k0 = pl.multiple_of(kb * BLK, BLK)
            new = []
            for h in range(heads):
                hs = slice(h * HEAD_DIM, (h + 1) * HEAD_DIM)
                p = jnp.exp2(scores[h, kb] * SCORE2 - tops[h])
                acc[hs, :] += dot_nn(vt[hs, pl.ds(k0, BLK)], p.astype(BF))
                new.append(ls[h] + jnp.sum(fold(p), axis=0))
            return tuple(new)

        ls = lax.fori_loop(first, end, mix_block, (jnp.zeros((8, BLK), F32),) * heads)
        for h in range(heads):
            hs = slice(h * HEAD_DIM, (h + 1) * HEAD_DIM)
            l = jnp.sum(ls[h], axis=0, keepdims=True)
            acc[hs, :] = acc[hs, :] * (1.0 / l)
            lse[h:h + 1, pl.ds(q0, BLK)] = tops[h] + jnp.log2(l)
        part = lax.bitwise_xor(lax.div(qb, per), scal[base])
        out[part, pl.ds(pl.multiple_of(lax.rem(qb, per) * BLK, BLK), BLK), :] = acc[...].T.astype(BF)
        return carry

    lax.fori_loop(0, nb, q_block, 0)


def attn_fwd(scal, xparts, wparts, bias, segk, segq):
    rows, d = xparts[0].shape
    t = 4 * rows
    width = wparts[0].shape[1] // 3
    heads = width // HEAD_DIM
    nb = t // BLK
    npc = len(wparts)
    anyspec = pl.BlockSpec(memory_space=pl.ANY)
    v = pl.BlockSpec(memory_space=pltpu.VMEM)
    return pl.pallas_call(
        functools.partial(attn_fwd_kernel, nb, npc),
        out_shape=(jax.ShapeDtypeStruct((4, rows, width), BF), jax.ShapeDtypeStruct((8, t), F32)),
        in_specs=[pl.BlockSpec(memory_space=pltpu.SMEM)] + [anyspec] * (4 + npc) + [v] * 3,
        out_specs=(v, v),
        scratch_shapes=[
            pltpu.VMEM((t, d), BF), pltpu.VMEM((d, 3 * width), BF), pltpu.VMEM((heads, t, HEAD_DIM), BF),
            pltpu.VMEM((width, t), BF), pltpu.VMEM((width, t), BF), pltpu.VMEM((width, BLK), F32),
            pltpu.VMEM((heads, nb, BLK, BLK), F32),
            pltpu.SemaphoreType.DMA((5,)),
        ],
        compiler_params=pltpu.CompilerParams(vmem_limit_bytes=VMEM_LIMIT),
        cost_estimate=cost(28),
        name="attention_forward",
    )(scal, *xparts, *wparts, bias, segk, segq)


def attn_bwd_kernel(nb, npc, groups, *refs):
    scal = refs[0]
    xparts = refs[1:5]
    wparts = refs[5:5 + npc]
    daparts = refs[5 + npc:9 + npc]
    a_saved, bias, segk, segq, lse, dx, dbias = refs[9 + npc:16 + npc]
    dw_out = refs[16 + npc:16 + npc + groups]
    xs, ws, qs, ks, vs, das, qt, kt, dat, delta, dqt, dall, dka, dva, dw, sems, osem = refs[16 + npc + groups:]
    heads = ks.shape[0]
    width = heads * HEAD_DIM
    rows = xparts[0].shape[0]
    base = 2 * nb
    wcopies = load_parts(scal, wparts, ws, base + 5, wparts[0].shape[0], sems.at[4], 0)
    xcopies = [load_parts(scal, [p], xs, base + i, rows, sems.at[i], 0)[0] for i, p in enumerate(xparts)]
    for c in wcopies:
        c.wait()
    for i in range(4):
        xcopies[i].wait()
        start = pl.multiple_of(scal[base + i] * rows, rows)
        at = pl.ds(start, rows)
        x = xs[at, :]
        y = dot_nn(x, ws[...])
        q = y[:, :width] + bias[0:1, :]
        qt[:, at] = q.T.astype(BF)
        ql = q.astype(BF)
        kf = y[:, width:2 * width]
        kt[:, at] = kf.T.astype(BF)
        kl = kf.astype(BF)
        vl = (y[:, 2 * width:] + bias[1:2, :]).astype(BF)
        dal = daparts[i][...]
        daf = dal.astype(F32).T
        dat[:, at] = daf.astype(BF)
        prod = daf * a_saved[i].astype(F32).T
        for h in range(heads):
            hs = slice(h * HEAD_DIM, (h + 1) * HEAD_DIM)
            qs[h, at, :] = ql[:, hs]
            ks[h, at, :] = kl[:, hs]
            vs[h, at, :] = vl[:, hs]
            das[h, at, :] = dal[:, hs]
            delta[h:h + 1, at] = jnp.sum(prod[hs, :], axis=0, keepdims=True)
    dqt[...] = jnp.zeros_like(dqt)

    def k_block(kb, carry):
        k0 = pl.multiple_of(kb * BLK, BLK)
        kat = pl.ds(k0, BLK)
        dka[...] = jnp.zeros_like(dka)
        dva[...] = jnp.zeros_like(dva)
        sk = segk[kat, :]

        def q_block(qb, c2):
            q0 = pl.multiple_of(qb * BLK, BLK)
            qat = pl.ds(q0, BLK)
            mask = sk == segq[:, qat]
            for h in range(heads):
                hs = slice(h * HEAD_DIM, (h + 1) * HEAD_DIM)
                s = dot_nn(ks[h, kat, :], qt[hs, qat])
                p = jnp.where(mask, jnp.exp2(s * SCORE2 - lse[h:h + 1, qat]), 0.0)
                dp = dot_nn(vs[h, kat, :], dat[hs, qat])
                dva[h] += dot_nn(p.astype(BF), das[h, qat, :])
                ds = (p * (dp - delta[h:h + 1, qat])).astype(BF)
                dka[h] += dot_nn(ds, qs[h, qat, :])
                dqt[hs, qat] += dot_nn(kt[hs, kat], ds)
            return c2

        lax.fori_loop(scal[kb], scal[nb + kb], q_block, 0)
        for h in range(heads):
            hs = slice(h * HEAD_DIM, (h + 1) * HEAD_DIM)
            dall[width + h * HEAD_DIM:width + (h + 1) * HEAD_DIM, kat] = (dka[h].T * SCORE).astype(BF)
            dall[2 * width + h * HEAD_DIM:2 * width + (h + 1) * HEAD_DIM, kat] = dva[h].T.astype(BF)
        return carry

    lax.fori_loop(0, nb, k_block, 0)
    dall[:width, :] = (dqt[...] * SCORE).astype(BF)
    dbias[0:1, :] = jnp.sum(dall[:width, :].astype(F32), axis=1)[None, :]
    dbias[1:2, :] = jnp.sum(dall[2 * width:, :].astype(F32), axis=1)[None, :]
    dw[...] = dot_nn(dall[...], xs[...]).T.astype(dw.dtype)
    rows_d, per = wparts[0].shape[0], npc // groups
    stores = []
    for p in range(npc):
        at = pl.ds(pl.multiple_of(scal[base + 5 + p] * rows_d, rows_d), rows_d)
        stores.append(pltpu.make_async_copy(dw.at[at], dw_out[p // per].at[p % per], osem))
        stores[-1].start()
    for i in range(4):
        start = pl.multiple_of(scal[base + i] * rows, rows)
        at = pl.ds(start, rows)
        dx[i] = dot_nt(dall[:, at].astype(F32).T.astype(BF), ws[...]).astype(BF)
    for copy in stores:
        copy.wait()


def attn_bwd(scal, xparts, wparts, daparts, a_saved, bias, segk, segq, lse, groups):
    rows, d = xparts[0].shape
    t = 4 * rows
    width = wparts[0].shape[1] // 3
    heads = width // HEAD_DIM
    nb = t // BLK
    npc = len(wparts)
    anyspec = pl.BlockSpec(memory_space=pl.ANY)
    v = pl.BlockSpec(memory_space=pltpu.VMEM)
    head_rows = pltpu.VMEM((heads, t, HEAD_DIM), BF)
    flat = pltpu.VMEM((width, t), BF)
    return pl.pallas_call(
        functools.partial(attn_bwd_kernel, nb, npc, groups),
        out_shape=(
            jax.ShapeDtypeStruct((4, rows, d), BF),
            jax.ShapeDtypeStruct((2, width), F32),
        ) + (jax.ShapeDtypeStruct((npc // groups, wparts[0].shape[0], 3 * width), BF),) * groups,
        in_specs=[pl.BlockSpec(memory_space=pltpu.SMEM)] + [anyspec] * (4 + npc) + [v] * 9,
        out_specs=(v, v) + (anyspec,) * groups,
        scratch_shapes=[
            pltpu.VMEM((t, d), BF), pltpu.VMEM((d, 3 * width), BF),
            head_rows, head_rows, head_rows, head_rows, flat, flat, flat,
            pltpu.VMEM((8, t), F32), pltpu.VMEM((width, t), F32), pltpu.VMEM((3 * width, t), BF),
            pltpu.VMEM((heads, BLK, HEAD_DIM), F32), pltpu.VMEM((heads, BLK, HEAD_DIM), F32),
            pltpu.VMEM((d, 3 * width), BF), pltpu.SemaphoreType.DMA((5,)), pltpu.SemaphoreType.DMA(()),
        ],
        compiler_params=pltpu.CompilerParams(vmem_limit_bytes=VMEM_LIMIT),
        cost_estimate=cost(55),
        name="attention_backward",
    )(scal, *xparts, *wparts, *daparts, a_saved, bias, segk, segq, lse)


EPSILON = 1e-05
SUB = 640


def normal_rows(hidden):
    centre = hidden - jnp.mean(hidden, axis=-1, keepdims=True)
    inverse = lax.rsqrt(jnp.mean(centre * centre, axis=-1, keepdims=True) + EPSILON)
    return centre * inverse, inverse


def norm_back(upstream, normal, inverse, gain_row):
    scaled = upstream * gain_row
    return inverse * (scaled - jnp.mean(scaled, axis=-1, keepdims=True) - normal * jnp.mean(scaled * normal, axis=-1, keepdims=True))


def gelu_share(u):
    return 0.5 * (1.0 + lax.erf(u * (1.0 / math.sqrt(2.0))))


def start_weights(scal, first, wo_parts, w1_parts, w2_parts, wo, w1, w2, sems):
    def spans(parts):
        rows = parts[0].shape[1]
        return [pl.ds(pl.multiple_of(scal[first + i] * rows, rows), rows) for i in range(len(parts))]
    by_block = [[] for _ in range(5)]
    for part, at in zip(wo_parts, spans(wo_parts)):
        by_block[0].append(pltpu.make_async_copy(part, wo.at[:, at], sems.at[0]))
    for z in range(4):
        for dest, parts in ((w1, w1_parts), (w2, w2_parts)):
            for part, at in zip(parts, spans(parts)):
                by_block[1 + z].append(pltpu.make_async_copy(part.at[z], dest.at[z, at], sems.at[1 + z]))
    for copies in by_block:
        for copy in copies:
            copy.start()
    return by_block


def wait_all(copies):
    for copy in copies:
        copy.wait()


def post_fwd_kernel(npc, last, *refs):
    scal = refs[0]
    a, hidden, vec, ub = refs[1:5]
    wo_parts, w1_parts, w2_parts = refs[5:5 + npc], refs[5 + npc:5 + 2 * npc], refs[5 + 2 * npc:5 + 3 * npc]
    rest = refs[5 + 3 * npc:]
    outs, (wo, w1, w2, xn2, sems) = rest[:-5], rest[-5:]
    h1, h2 = outs[:2]
    loads = start_weights(scal, 1, wo_parts, w1_parts, w2_parts, wo, w1, w2, sems)
    wait_all(loads[0])
    total = hidden[...] + vec[4:5, :]
    for i in range(4):
        total += dot_nt(a[i], wo[lax.bitwise_xor(i, scal[0])])
    h1[...] = total
    normal, _ = normal_rows(total)
    xn2[...] = (normal * vec[2:3, :] + vec[3:4, :]).astype(BF)
    h2[...] = total + vec[5:6, :]
    units = w1.shape[2]
    for z in range(4):
        wait_all(loads[1 + z])

        def step(j, carry):
            at = pl.ds(pl.multiple_of(j * SUB, SUB), SUB)
            u = dot_nn(xn2[...], w1[z, :, at]) + ub[z, :, at]
            g = (u * gelu_share(u)).astype(BF)
            h2[...] += dot_nt(g, w2[z, :, at])
            return carry

        lax.fori_loop(0, units // SUB, step, 0)
    if not last:
        normal, _ = normal_rows(h2[...])
        outs[2][...] = (normal * vec[8:9, :] + vec[9:10, :]).astype(BF)


def post_fwd(scal, a, hidden, vec, ub, wo_parts, w1_parts, w2_parts, last):
    rows, d = hidden.shape
    npc = len(w1_parts)
    width, units = wo_parts[0].shape[2], w1_parts[0].shape[2]
    anyspec = pl.BlockSpec(memory_space=pl.ANY)
    v = pl.BlockSpec(memory_space=pltpu.VMEM)
    out = [jax.ShapeDtypeStruct((rows, d), F32)] * 2 + ([] if last else [jax.ShapeDtypeStruct((rows, d), BF)])
    return pl.pallas_call(
        functools.partial(post_fwd_kernel, npc, last),
        out_shape=out,
        in_specs=[pl.BlockSpec(memory_space=pltpu.SMEM)] + [v] * 4 + [anyspec] * (3 * npc),
        out_specs=[v] * len(out),
        scratch_shapes=[
            pltpu.VMEM((4, d, width), BF), pltpu.VMEM((4, d, units), BF), pltpu.VMEM((4, d, units), BF),
            pltpu.VMEM((rows, d), BF), pltpu.SemaphoreType.DMA((5,)),
        ],
        compiler_params=pltpu.CompilerParams(vmem_limit_bytes=VMEM_LIMIT),
        cost_estimate=cost(16),
        name="rows_forward",
    )(scal, a, hidden, vec, ub, *wo_parts, *w1_parts, *w2_parts)


def post_bwd_kernel(npc, groups, *refs):
    scal = refs[0]
    a, h1, gy, vec, ub = refs[1:6]
    wo_parts, w1_parts, w2_parts = refs[6:6 + npc], refs[6 + npc:6 + 2 * npc], refs[6 + 2 * npc:6 + 3 * npc]
    rest = refs[6 + 3 * npc:]
    gy1, da_out, dub, dvec = rest[:4]
    dwo_out, dw1_out, dw2_out = rest[4:4 + groups], rest[4 + groups:4 + 2 * groups], rest[4 + 2 * groups:4 + 3 * groups]
    wo, w1, w2, dwo, dw1, dw2, xn2, df, xn2t, dft, dxn2, sems, osem = rest[4 + 3 * groups:]
    loads = start_weights(scal, 1, wo_parts, w1_parts, w2_parts, wo, w1, w2, sems)
    per = npc // groups
    rows_d = w1_parts[0].shape[1]
    spans = [pl.ds(pl.multiple_of(scal[1 + i] * rows_d, rows_d), rows_d) for i in range(npc)]
    normal, inverse = normal_rows(h1[...])
    xlow = (normal * vec[2:3, :] + vec[3:4, :]).astype(BF)
    xn2[...] = xlow
    xn2t[...] = xlow.T
    low = gy[...].astype(BF)
    df[...] = low
    dft[...] = low.T
    dvec[...] = jnp.zeros_like(dvec)
    dvec[5:6, :] = jnp.sum(low.astype(F32), axis=0, keepdims=True)
    dxn2[...] = jnp.zeros_like(dxn2)
    units = w1.shape[2]
    stores = []
    for z in range(4):
        wait_all(loads[1 + z])

        def step(j, carry):
            at = pl.ds(pl.multiple_of(j * SUB, SUB), SUB)
            u = dot_nn(xn2[...], w1[z, :, at]) + ub[z, :, at]
            share = gelu_share(u)
            g = (u * share).astype(BF)
            dg = dot_nn(df[...], w2[z, :, at])
            slope = share + u * jnp.exp(-0.5 * u * u) * (1.0 / math.sqrt(2.0 * math.pi))
            du = (dg * slope).astype(BF)
            dub[z, :, at] = jnp.sum(du.astype(F32), axis=0, keepdims=True)
            dw1[z, :, at] = dot_nn(xn2t[...], du).astype(BF)
            dw2[z, :, at] = dot_nn(dft[...], g).astype(BF)
            dxn2[...] += dot_nt(du, w1[z, :, at])
            return carry

        lax.fori_loop(0, units // SUB, step, 0)
        for p in range(npc):
            for src, outs in ((dw1, dw1_out), (dw2, dw2_out)):
                stores.append(pltpu.make_async_copy(src.at[z, spans[p]], outs[p // per].at[p % per, z], osem))
                stores[-1].start()
    wait_all(loads[0])
    upstream = dxn2[...]
    dvec[2:3, :] = jnp.sum(upstream * normal, axis=0, keepdims=True)
    dvec[3:4, :] = jnp.sum(upstream, axis=0, keepdims=True)
    total = gy[...] + norm_back(upstream, normal, inverse, vec[2:3, :])
    gy1[...] = total
    low = total.astype(BF)
    dvec[4:5, :] = jnp.sum(low.astype(F32), axis=0, keepdims=True)
    dat = low.T
    for i in range(4):
        slot = lax.bitwise_xor(i, scal[0])
        dwo[slot] = dot_nn(dat, a[i]).astype(BF)
        da_out[i] = dot_nn(low, wo[slot]).astype(BF)
    for p in range(npc):
        stores.append(pltpu.make_async_copy(dwo.at[:, spans[p]], dwo_out[p // per].at[p % per], osem))
        stores[-1].start()
    wait_all(stores)


def post_bwd(scal, a, h1, gy, vec, ub, wo_parts, w1_parts, w2_parts, groups):
    rows, d = h1.shape
    npc = len(w1_parts)
    per = npc // groups
    rows_d, width, units = wo_parts[0].shape[1], wo_parts[0].shape[2], w1_parts[0].shape[2]
    anyspec = pl.BlockSpec(memory_space=pl.ANY)
    v = pl.BlockSpec(memory_space=pltpu.VMEM)
    out = [jax.ShapeDtypeStruct((rows, d), F32), jax.ShapeDtypeStruct((4, rows, width), BF),
           jax.ShapeDtypeStruct((4, 1, units), F32), jax.ShapeDtypeStruct((8, d), F32)]
    out += [jax.ShapeDtypeStruct((per, 4, rows_d, width), BF)] * groups
    out += [jax.ShapeDtypeStruct((per, 4, rows_d, units), BF)] * (2 * groups)
    return pl.pallas_call(
        functools.partial(post_bwd_kernel, npc, groups),
        out_shape=out,
        in_specs=[pl.BlockSpec(memory_space=pltpu.SMEM)] + [v] * 5 + [anyspec] * (3 * npc),
        out_specs=[v] * 4 + [anyspec] * (3 * groups),
        scratch_shapes=[
            pltpu.VMEM((4, d, width), BF), pltpu.VMEM((4, d, units), BF), pltpu.VMEM((4, d, units), BF),
            pltpu.VMEM((4, d, width), BF), pltpu.VMEM((4, d, units), BF), pltpu.VMEM((4, d, units), BF),
            pltpu.VMEM((rows, d), BF), pltpu.VMEM((rows, d), BF), pltpu.VMEM((d, rows), BF), pltpu.VMEM((d, rows), BF),
            pltpu.VMEM((rows, d), F32), pltpu.SemaphoreType.DMA((5,)), pltpu.SemaphoreType.DMA(()),
        ],
        compiler_params=pltpu.CompilerParams(vmem_limit_bytes=VMEM_LIMIT),
        cost_estimate=cost(33),
        name="rows_backward",
    )(scal, a, h1, gy, vec, ub, *wo_parts, *w1_parts, *w2_parts)


MOMENTUM = 0.9
AVERAGE_KEEP = 0.9
WEIGHT_DECAY = 0.0001
RATE_SCALE = 0.02
ROWS_AXES = ("y", "x", "c")
COLS_AXES = ("h", "b")
EVERY = ROWS_AXES + COLS_AXES


def swap(value, name):
    return lax.ppermute(value, name, [(0, 1), (1, 0)])


def home(value):
    return lax.ppermute(value, ("c", "h"), [(0, 0), (1, 2), (2, 1), (3, 3)])


def corner(value):
    return lax.ppermute(value, ("c", "b"), [(0, 3), (1, 2), (2, 1), (3, 0)])


def double(value, name):
    return jnp.concatenate([value, swap(value, name)], axis=0)


def plane_parts(value, x_first):
    across = swap(value, "x")
    along = swap(value, "y")
    both = swap(across, "y") if x_first else swap(along, "x")
    return [value, across, along, both]


def core_parts(parts):
    return parts + [swap(part, "c") for part in parts]


def f32(value):
    return value.astype(F32)


def reduce_plane(terms, x_first):
    def pick(dy, dx):
        return sum(f32(t[2 * dy + dx]) for t in terms)

    if x_first:
        got = swap(jnp.stack([pick(0, 1), pick(1, 1)]).astype(BF), "x")
        got2 = swap((pick(1, 0) + f32(got[1])).astype(BF), "y")
    else:
        got = swap(jnp.stack([pick(1, 0), pick(1, 1)]).astype(BF), "y")
        got2 = swap((pick(0, 1) + f32(got[1])).astype(BF), "x")
    return lambda index: pick(0, 0)[index] + f32(got[0][index]) + f32(got2[index])


def reduce_line(take):
    got = swap(take(slice(2, 4)).astype(BF), "h")
    got2 = swap((take(1) + f32(got[1])).astype(BF), "b")
    return take(0) + f32(got[0]) + f32(got2)


def sgd_step(weight, gradient, moment, average, step_rate):
    decayed = gradient + WEIGHT_DECAY * weight
    moment_next = MOMENTUM * moment + decayed
    weight_next = weight - step_rate * (decayed + MOMENTUM * moment_next)
    average_next = AVERAGE_KEEP * average + (1.0 - AVERAGE_KEEP) * weight_next
    return (weight_next, moment_next, average_next)


def local(
    tokens_in, cotangent, lengths, segments, bucket_map, bucket_tokens,
    attention, feedforward, vectors, head_bias, unit_bias,
    attention_moment, feedforward_moment, vectors_moment, head_moment, unit_moment,
    attention_mean, feedforward_mean, vectors_mean, head_mean, unit_mean,
):
    rows, width_d = tokens_in.shape
    layer_count = attention.shape[0]
    iy, ix, ic, ih, ib = (lax.axis_index(name) for name in EVERY)
    x_size = lax.axis_size("x")
    fast = lax.axis_size("y") == 2 and x_size == 2
    dp_size = lax.axis_size("y") * x_size * 2
    dp_place = (iy * x_size + ix) * 2 + ic
    mp_place = 2 * ih + ib
    quarter = 2 * ic + ib
    stays = ic == ih
    pack_length = rows * 4
    nb = pack_length // BLK

    low_attention, low_feedforward, low_vectors, low_head, low_unit = lax.optimization_barrier(
        tuple(p.astype(BF) for p in (attention, feedforward, vectors, head_bias, unit_bias))
    )

    hidden_low = home(tokens_in)
    meta = jnp.concatenate([segments[0], jnp.sum(lengths[0])[None], bucket_map])
    meta = jnp.where(stays, meta, swap(meta, "c"))
    segment_row, total_live, bucket = meta[:pack_length], meta[pack_length], meta[pack_length + 1]

    if fast:
        v8 = double(double(double(low_vectors.reshape(1, layer_count * 6, -1), "c"), "x"), "y")
        v8 = v8.reshape(2, 2, 2, layer_count * 6, -1)
        for axis, place in ((0, iy), (1, ix), (2, ic)):
            v8 = jnp.where(place == 1, jnp.flip(v8, axis), v8)
        full_vectors = v8.reshape(8, layer_count * 6, -1).transpose(1, 0, 2).reshape(layer_count, 6, width_d)
        units4 = double(double(low_unit[None], "b"), "h")
        heads_used = jnp.where(stays, low_head, swap(low_head, "h"))
        qkv_parts, wo_parts, up_parts, down_parts = [], [], [], []
        for layer in range(layer_count):
            qkv = jnp.concatenate([low_attention[layer, i] for i in range(3)], axis=1)
            far = swap(qkv, "h")
            mine = plane_parts(jnp.where(stays, qkv, far), True)
            theirs = plane_parts(jnp.where(stays, far, qkv), False)
            qkv_parts.append(mine + [swap(part, "c") for part in theirs])
            wo_parts.append(core_parts(plane_parts(double(double(low_attention[layer, 3][None], "b"), "h"), layer % 2 == 0)))
            up_parts.append(core_parts(plane_parts(double(double(low_feedforward[layer, 0][None], "b"), "h"), True)))
            down_parts.append(core_parts(plane_parts(double(double(low_feedforward[layer, 1][None], "b"), "h"), False)))
        chunk_places = [dp_place ^ (2 * (p % 4) + p // 4) for p in range(8)]
        switch = 2 * (ic ^ ih)
        groups = 2
    else:
        full_vectors = lax.all_gather(low_vectors, ROWS_AXES, axis=2, tiled=True)
        units4 = lax.all_gather(low_unit, COLS_AXES, axis=0)
        heads_used = lax.all_gather(low_head, COLS_AXES, axis=0)[quarter]
        whole_attention = lax.all_gather(lax.all_gather(low_attention, ROWS_AXES, axis=2, tiled=True), COLS_AXES, axis=0)
        whole_feedforward = lax.all_gather(lax.all_gather(low_feedforward, ROWS_AXES, axis=2, tiled=True), COLS_AXES, axis=0)
        own = whole_attention[quarter]
        qkv_parts = [[jnp.concatenate([own[layer, i] for i in range(3)], axis=1)] for layer in range(layer_count)]
        wo_parts = [[whole_attention[:, layer, 3]] for layer in range(layer_count)]
        up_parts = [[whole_feedforward[:, layer, 0]] for layer in range(layer_count)]
        down_parts = [[whole_feedforward[:, layer, 1]] for layer in range(layer_count)]
        chunk_places = [jnp.int32(0)]
        switch = quarter
        groups = 1
    vec = f32(full_vectors)
    unit_rows = f32(units4)
    head_rows = f32(heads_used)

    positions = jnp.arange(pack_length, dtype=jnp.int32)
    own_segment = jnp.where(positions < total_live, segment_row, 64 + positions)
    by_block = own_segment.reshape(nb, BLK)
    first_block = jnp.sum(own_segment[None, :] < by_block[:, :1], axis=1) // BLK
    end_block = (jnp.sum(own_segment[None, :] <= by_block[:, -1:], axis=1) + BLK - 1) // BLK
    places = jnp.stack([quarter ^ rel for rel in range(4)])
    chunk_array = jnp.stack(chunk_places).astype(jnp.int32)
    scal = jnp.concatenate([first_block, end_block, places, jnp.zeros((1,), jnp.int32), chunk_array]).astype(jnp.int32)
    scal_rows = jnp.concatenate([jnp.reshape(switch, (1,)).astype(jnp.int32), chunk_array])
    segk, segq = own_segment[:, None], own_segment[None, :]
    live_own = (quarter * rows + jnp.arange(rows) < total_live)[:, None]
    counts_float = f32(bucket_tokens)
    chosen = jnp.arange(bucket_tokens.shape[0]) == bucket
    pack_weight = bucket_tokens.shape[0] * jnp.sum(jnp.where(chosen, counts_float, 0.0)) / jnp.sum(counts_float)

    def vec_rows(layer, other):
        return jnp.concatenate([vec[layer], jnp.zeros((2, width_d), F32), vec[other], jnp.zeros((2, width_d), F32)])

    hidden = f32(hidden_low)
    normal, _ = normal_rows(hidden)
    normed = (normal * vec[0, 0] + vec[0, 1]).astype(BF)
    saved = []
    for layer in range(layer_count):
        last = layer == layer_count - 1
        over = swap(normed, "b")
        normed_parts = [normed, over, swap(normed, "c"), swap(over, "c")]
        mixed, log_total = attn_fwd(scal, normed_parts, qkv_parts[layer], head_rows[layer], segk, segq)
        own_mixed = jnp.stack([mixed[0], swap(mixed[1], "b"), swap(mixed[2], "c"), corner(mixed[3])])
        unit_row = unit_rows[:, layer][:, None, :]
        vec16 = vec_rows(layer, 0 if last else layer + 1)
        outs = post_fwd(scal_rows, own_mixed, hidden, vec16, unit_row, wo_parts[layer], up_parts[layer], down_parts[layer], last)
        saved.append((hidden, normed_parts, mixed, log_total, own_mixed, outs[0], unit_row, vec16))
        hidden = outs[1]
        if not last:
            normed = outs[2]
    hidden_out = home(jnp.where(live_own, hidden, 0.0))

    upstream = jnp.where(live_own, f32(home(cotangent)) * pack_weight, 0.0)
    attention_grads, feedforward_grads, vector_grads, head_grads, unit_grads = [], [], [], [], []
    for layer in reversed(range(layer_count)):
        hidden, normed_parts, mixed, log_total, own_mixed, middle, unit_row, vec16 = saved[layer]
        outs = post_bwd(scal_rows, own_mixed, middle, upstream, vec16, unit_row, wo_parts[layer], up_parts[layer], down_parts[layer], groups)
        upstream, d_mixed, d_unit, d_vec = outs[:4]
        d_wo, d_up, d_down = outs[4:4 + groups], outs[4 + groups:4 + 2 * groups], outs[4 + 2 * groups:4 + 3 * groups]
        d_parts = [d_mixed[0], swap(d_mixed[1], "b"), swap(d_mixed[2], "c"), corner(d_mixed[3])]
        outs = attn_bwd(scal, normed_parts, qkv_parts[layer], d_parts, mixed, head_rows[layer], segk, segq, log_total, groups)
        d_rows, d_head = outs[:2]
        d_qkv = outs[2:]
        got = swap(d_rows[2:4], "c")
        got2 = swap((f32(d_rows[1]) + f32(got[1])).astype(BF), "b")
        d_normed = f32(d_rows[0]) + f32(got[0]) + f32(got2)
        normal, inverse = normal_rows(hidden)
        upstream = upstream + norm_back(d_normed, normal, inverse, vec[layer, 0])
        vector_grads.append(jnp.concatenate([
            jnp.sum(d_normed * normal, axis=0)[None], jnp.sum(d_normed, axis=0)[None], d_vec[2:6]]))
        head_grads.append(d_head)
        unit_grads.append(d_unit[:, 0])
        if fast:
            up_grad, down_grad, wo_grad = (
                reduce_line(reduce_plane([keep, swap(send, "c")], x_first))
                for (keep, send), x_first in ((d_up, False), (d_down, True), (d_wo, layer % 2 == 0))
            )
            other = swap(d_qkv[1], "c")
            near = jnp.where(stays, d_qkv[0], other)
            far = jnp.where(stays, other, d_qkv[0])
            take = reduce_plane([jnp.stack([near, far], axis=1)], layer % 2 == 0)
            qkv_grad = take(0) + f32(swap(take(1).astype(BF), "h"))
        else:
            def scatter(value):
                value = lax.psum_scatter(f32(value), COLS_AXES, scatter_dimension=0, tiled=True)[0]
                return lax.psum_scatter(value, ROWS_AXES, scatter_dimension=0, tiled=True)

            up_grad, down_grad, wo_grad = scatter(d_up[0][0]), scatter(d_down[0][0]), scatter(d_wo[0][0])
            empty = jnp.zeros((4,) + d_qkv[0].shape[1:], F32)
            qkv_grad = scatter(empty.at[quarter].set(f32(d_qkv[0][0])))
        head_width = attention.shape[3]
        attention_grads.append(jnp.stack([qkv_grad[:, i * head_width:(i + 1) * head_width] for i in range(3)] + [wo_grad]))
        feedforward_grads.append(jnp.stack([up_grad, down_grad]))
    attention_gradient = jnp.stack(attention_grads[::-1])
    feedforward_gradient = jnp.stack(feedforward_grads[::-1])

    vector_sum = jnp.stack(vector_grads[::-1])
    head_sum = jnp.stack(head_grads[::-1])
    unit_sum = jnp.stack(unit_grads[::-1], axis=1)
    v_size, u_size, e_size = vector_sum.size, unit_sum.size // 4, head_sum.size
    if fast:
        flat_v, flat_e = vector_sum.reshape(-1), head_sum.reshape(-1)
        flat_u = unit_sum.reshape(4, -1)
        near = jnp.where(stays, flat_e, 0.0)
        got = swap(jnp.concatenate([flat_v, flat_u[2], flat_u[3], flat_e - near]), "h")
        flat_v = flat_v + got[:v_size]
        flat_e = near + got[v_size + 2 * u_size:]
        near_u = flat_u[0] + got[v_size:v_size + u_size]
        got2 = swap(jnp.concatenate([flat_v, flat_u[1] + got[v_size + u_size:v_size + 2 * u_size]]), "b")
        flat = jnp.concatenate([flat_v + got2[:v_size], near_u + got2[v_size:], flat_e])
        for name in ROWS_AXES:
            flat = flat + swap(flat, name)
        vector_total = flat[:v_size].reshape(vector_sum.shape)
        unit_gradient = flat[v_size:v_size + u_size].reshape(unit_bias.shape)
        head_gradient = flat[v_size + u_size:].reshape(head_bias.shape)
    else:
        placed = jnp.zeros((4,) + head_sum.shape, F32).at[quarter].set(head_sum)
        vector_total, unit_total, head_total = lax.psum((vector_sum, unit_sum, placed), EVERY)
        unit_gradient, head_gradient = unit_total[mp_place], head_total[mp_place]
    chunk = width_d // dp_size
    vectors_gradient = lax.dynamic_slice_in_dim(vector_total, dp_place * chunk, chunk, 2)

    input_gradient = f32(home(upstream.astype(BF)))
    input_gradient = jnp.where(stays, upstream, input_gradient)
    step_rate = RATE_SCALE * lax.rsqrt(jnp.float32(dp_size * pack_length))
    weights = (attention, feedforward, vectors, head_bias, unit_bias)
    gradients = (attention_gradient, feedforward_gradient, vectors_gradient, head_gradient, unit_gradient)
    moments = (attention_moment, feedforward_moment, vectors_moment, head_moment, unit_moment)
    averages = (attention_mean, feedforward_mean, vectors_mean, head_mean, unit_mean)
    steps = [sgd_step(*leaf, step_rate) for leaf in zip(weights, gradients, moments, averages)]
    return (
        (hidden_out, input_gradient) + gradients + tuple(s[0] for s in steps) + tuple(s[1] for s in steps)
        + tuple(s[2] for s in steps) + (steps[0][0].astype(BF), steps[1][0].astype(BF))
    )


def solution(mesh):
    dp_size = mesh.shape["dp"]
    inner = jax.sharding.Mesh(mesh.devices.reshape(2, dp_size // 4, 2, 2, 2), EVERY)
    rows, cols = ROWS_AXES, COLS_AXES
    tokens = P(rows + cols, None)
    params = (P(None, None, rows, cols), P(None, None, rows, cols), P(None, None, rows), P(None, None, cols), P(None, cols))
    in_specs = (tokens, tokens, P(rows, None), P(rows, None), P(rows), P()) + params * 3
    out_specs = (tokens, tokens) + params * 4 + params[:2]
    return jax.shard_map(local, mesh=inner, in_specs=in_specs, out_specs=out_specs, check_vma=False)
```

```python
import functools, math
import jax, jax.numpy as jnp
from jax import lax
from jax.experimental import pallas as pl
from jax.experimental.pallas import tpu as pltpu
from jax.sharding import PartitionSpec as P

HEAD_DIM = 32
MASKED = -1e30
LOG2E = math.log2(math.e)
SCORE = HEAD_DIM ** (-0.5)
SCORE2 = SCORE * LOG2E
BLK = 256
BF = jnp.bfloat16
F32 = jnp.float32
VMEM_LIMIT = 60 * 1024 * 1024


def cost(micros):
    return pl.CostEstimate(flops=micros * 1100000000, bytes_accessed=1000000, transcendentals=0)


def dot_nn(a, b):
    return lax.dot_general(a, b, (((1,), (0,)), ((), ())), preferred_element_type=F32)


def dot_nt(a, b):
    return lax.dot_general(a, b, (((1,), (1,)), ((), ())), preferred_element_type=F32)


def load_parts(scal, parts, dest, first, rows, sem):
    copies = []
    for i, part in enumerate(parts):
        start = pl.multiple_of(scal[first + i] * rows, rows)
        copies.append(pltpu.make_async_copy(part, dest.at[pl.ds(start, rows)], sem))
    for copy in copies:
        copy.start()
    return copies


def chunks_of(wrefs, layer):
    return [w.at[core, layer] for core in range(wrefs[0].shape[0]) for w in wrefs]


def attn_fwd_kernel(nb, nw, layer, *refs):
    scal = refs[0]
    xparts = refs[1:5]
    wparts = chunks_of(refs[5:5 + nw], layer)
    bias, segk, segq, out, lse = refs[5 + nw:10 + nw]
    xs, ws, ks, qt, vt, acc, scores, sems = refs[10 + nw:]
    heads = ks.shape[0]
    width = heads * HEAD_DIM
    rows = xparts[0].shape[0]
    base = 2 * nb
    wcopies = load_parts(scal, wparts, ws, base + 5, wparts[0].shape[0], sems.at[4])
    xcopies = [load_parts(scal, [p], xs, base + i, rows, sems.at[i])[0] for i, p in enumerate(xparts)]
    for c in wcopies:
        c.wait()
    for i in range(4):
        xcopies[i].wait()
        start = pl.multiple_of(scal[base + i] * rows, rows)
        y = dot_nn(xs[pl.ds(start, rows), :], ws[...])
        qt[:, pl.ds(start, rows)] = (y[:, :width] + bias[0:1, :]).T.astype(BF)
        k = y[:, width:2 * width].astype(BF)
        for h in range(heads):
            ks[h, pl.ds(start, rows), :] = k[:, h * HEAD_DIM:(h + 1) * HEAD_DIM]
        vt[:, pl.ds(start, rows)] = (y[:, 2 * width:] + bias[1:2, :]).T.astype(BF)
    lse[...] = jnp.zeros_like(lse)
    per = rows // BLK

    def fold(z):
        return z.reshape(BLK // 8, 8, BLK)

    def q_block(qb, carry):
        q0 = pl.multiple_of(qb * BLK, BLK)
        acc[...] = jnp.zeros_like(acc)
        sq = segq[:, pl.ds(q0, BLK)]
        first, end = scal[qb], scal[nb + qb]

        def score_block(kb, ms):
            k0 = pl.multiple_of(kb * BLK, BLK)
            mask = segk[pl.ds(k0, BLK), :] == sq
            new = []
            for h in range(heads):
                hs = slice(h * HEAD_DIM, (h + 1) * HEAD_DIM)
                s = dot_nn(ks[h, pl.ds(k0, BLK), :], qt[hs, pl.ds(q0, BLK)])
                s = jnp.where(mask, s, MASKED)
                scores[h, kb] = s
                new.append(jnp.maximum(ms[h], jnp.max(fold(s), axis=0)))
            return tuple(new)

        ms = lax.fori_loop(first, end, score_block, (jnp.full((8, BLK), MASKED, F32),) * heads)
        tops = [jnp.max(m, axis=0, keepdims=True) * SCORE2 for m in ms]

        def mix_block(kb, ls):
            k0 = pl.multiple_of(kb * BLK, BLK)
            new = []
            for h in range(heads):
                hs = slice(h * HEAD_DIM, (h + 1) * HEAD_DIM)
                p = jnp.exp2(scores[h, kb] * SCORE2 - tops[h])
                acc[hs, :] += dot_nn(vt[hs, pl.ds(k0, BLK)], p.astype(BF))
                new.append(ls[h] + jnp.sum(fold(p), axis=0))
            return tuple(new)

        ls = lax.fori_loop(first, end, mix_block, (jnp.zeros((8, BLK), F32),) * heads)
        for h in range(heads):
            hs = slice(h * HEAD_DIM, (h + 1) * HEAD_DIM)
            l = jnp.sum(ls[h], axis=0, keepdims=True)
            acc[hs, :] = acc[hs, :] * (1.0 / l)
            lse[h:h + 1, pl.ds(q0, BLK)] = tops[h] + jnp.log2(l)
        part = lax.bitwise_xor(lax.div(qb, per), scal[base])
        out[part, pl.ds(pl.multiple_of(lax.rem(qb, per) * BLK, BLK), BLK), :] = acc[...].T.astype(BF)
        return carry

    lax.fori_loop(0, nb, q_block, 0)


def attn_fwd(scal, xparts, wparts, layer, bias, segk, segq):
    rows, d = xparts[0].shape
    t = 4 * rows
    width = wparts[0].shape[3] // 3
    heads = width // HEAD_DIM
    nb = t // BLK
    npc = len(wparts)
    anyspec = pl.BlockSpec(memory_space=pl.ANY)
    v = pl.BlockSpec(memory_space=pltpu.VMEM)
    return pl.pallas_call(
        functools.partial(attn_fwd_kernel, nb, npc, layer),
        out_shape=(jax.ShapeDtypeStruct((4, rows, width), BF), jax.ShapeDtypeStruct((8, t), F32)),
        in_specs=[pl.BlockSpec(memory_space=pltpu.SMEM)] + [anyspec] * (4 + npc) + [v] * 3,
        out_specs=(v, v),
        scratch_shapes=[
            pltpu.VMEM((t, d), BF), pltpu.VMEM((d, 3 * width), BF), pltpu.VMEM((heads, t, HEAD_DIM), BF),
            pltpu.VMEM((width, t), BF), pltpu.VMEM((width, t), BF), pltpu.VMEM((width, BLK), F32),
            pltpu.VMEM((heads, nb, BLK, BLK), F32),
            pltpu.SemaphoreType.DMA((5,)),
        ],
        compiler_params=pltpu.CompilerParams(vmem_limit_bytes=VMEM_LIMIT),
        cost_estimate=cost(28),
        name="attention_forward",
    )(scal, *xparts, *wparts, bias, segk, segq)


def attn_bwd_kernel(nb, nw, layer, *refs):
    scal = refs[0]
    xparts = refs[1:5]
    groups = refs[5].shape[0]
    wparts = chunks_of(refs[5:5 + nw], layer)
    npc = len(wparts)
    daparts = refs[5 + nw:9 + nw]
    a_saved, bias, segk, segq, lse, dx, dbias = refs[9 + nw:16 + nw]
    dw_out = refs[16 + nw:16 + nw + groups]
    xs, ws, qs, ks, vs, das, qt, kt, dat, delta, dqt, dall, dka, dva, dw, sems, osem = refs[16 + nw + groups:]
    heads = ks.shape[0]
    width = heads * HEAD_DIM
    rows = xparts[0].shape[0]
    base = 2 * nb
    wcopies = load_parts(scal, wparts, ws, base + 5, wparts[0].shape[0], sems.at[4])
    xcopies = [load_parts(scal, [p], xs, base + i, rows, sems.at[i])[0] for i, p in enumerate(xparts)]
    for c in wcopies:
        c.wait()
    for i in range(4):
        xcopies[i].wait()
        start = pl.multiple_of(scal[base + i] * rows, rows)
        at = pl.ds(start, rows)
        x = xs[at, :]
        y = dot_nn(x, ws[...])
        q = y[:, :width] + bias[0:1, :]
        qt[:, at] = q.T.astype(BF)
        ql = q.astype(BF)
        kf = y[:, width:2 * width]
        kt[:, at] = kf.T.astype(BF)
        kl = kf.astype(BF)
        vl = (y[:, 2 * width:] + bias[1:2, :]).astype(BF)
        dal = daparts[i][...]
        daf = dal.astype(F32).T
        dat[:, at] = daf.astype(BF)
        prod = daf * a_saved[i].astype(F32).T
        for h in range(heads):
            hs = slice(h * HEAD_DIM, (h + 1) * HEAD_DIM)
            qs[h, at, :] = ql[:, hs]
            ks[h, at, :] = kl[:, hs]
            vs[h, at, :] = vl[:, hs]
            das[h, at, :] = dal[:, hs]
            delta[h:h + 1, at] = jnp.sum(prod[hs, :], axis=0, keepdims=True)
    dqt[...] = jnp.zeros_like(dqt)

    def k_block(kb, carry):
        k0 = pl.multiple_of(kb * BLK, BLK)
        kat = pl.ds(k0, BLK)
        dka[...] = jnp.zeros_like(dka)
        dva[...] = jnp.zeros_like(dva)
        sk = segk[kat, :]

        def q_block(qb, c2):
            q0 = pl.multiple_of(qb * BLK, BLK)
            qat = pl.ds(q0, BLK)
            mask = sk == segq[:, qat]
            for h in range(heads):
                hs = slice(h * HEAD_DIM, (h + 1) * HEAD_DIM)
                s = dot_nn(ks[h, kat, :], qt[hs, qat])
                p = jnp.where(mask, jnp.exp2(s * SCORE2 - lse[h:h + 1, qat]), 0.0)
                dp = dot_nn(vs[h, kat, :], dat[hs, qat])
                dva[h] += dot_nn(p.astype(BF), das[h, qat, :])
                ds = (p * (dp - delta[h:h + 1, qat])).astype(BF)
                dka[h] += dot_nn(ds, qs[h, qat, :])
                dqt[hs, qat] += dot_nn(kt[hs, kat], ds)
            return c2

        lax.fori_loop(scal[kb], scal[nb + kb], q_block, 0)
        for h in range(heads):
            hs = slice(h * HEAD_DIM, (h + 1) * HEAD_DIM)
            dall[width + h * HEAD_DIM:width + (h + 1) * HEAD_DIM, kat] = (dka[h].T * SCORE).astype(BF)
            dall[2 * width + h * HEAD_DIM:2 * width + (h + 1) * HEAD_DIM, kat] = dva[h].T.astype(BF)
        return carry

    lax.fori_loop(0, nb, k_block, 0)
    dall[:width, :] = (dqt[...] * SCORE).astype(BF)
    dbias[0:1, :] = jnp.sum(dall[:width, :].astype(F32), axis=1)[None, :]
    dbias[1:2, :] = jnp.sum(dall[2 * width:, :].astype(F32), axis=1)[None, :]
    dw[...] = dot_nn(dall[...], xs[...]).T.astype(dw.dtype)
    rows_d, per = wparts[0].shape[0], npc // groups
    stores = []
    for p in range(npc):
        at = pl.ds(pl.multiple_of(scal[base + 5 + p] * rows_d, rows_d), rows_d)
        stores.append(pltpu.make_async_copy(dw.at[at], dw_out[p // per].at[p % per], osem))
        stores[-1].start()
    for i in range(4):
        start = pl.multiple_of(scal[base + i] * rows, rows)
        at = pl.ds(start, rows)
        dx[i] = dot_nt(dall[:, at].astype(F32).T.astype(BF), ws[...]).astype(BF)
    for copy in stores:
        copy.wait()


def attn_bwd(scal, xparts, wparts, layer, daparts, a_saved, bias, segk, segq, lse):
    rows, d = xparts[0].shape
    t = 4 * rows
    groups, _, rows_w, width = wparts[0].shape
    width //= 3
    heads = width // HEAD_DIM
    nb = t // BLK
    npc = len(wparts)
    anyspec = pl.BlockSpec(memory_space=pl.ANY)
    v = pl.BlockSpec(memory_space=pltpu.VMEM)
    head_rows = pltpu.VMEM((heads, t, HEAD_DIM), BF)
    flat = pltpu.VMEM((width, t), BF)
    return pl.pallas_call(
        functools.partial(attn_bwd_kernel, nb, npc, layer),
        out_shape=(
            jax.ShapeDtypeStruct((4, rows, d), BF),
            jax.ShapeDtypeStruct((2, width), F32),
        ) + (jax.ShapeDtypeStruct((npc, rows_w, 3 * width), BF),) * groups,
        in_specs=[pl.BlockSpec(memory_space=pltpu.SMEM)] + [anyspec] * (4 + npc) + [v] * 9,
        out_specs=(v, v) + (anyspec,) * groups,
        scratch_shapes=[
            pltpu.VMEM((t, d), BF), pltpu.VMEM((d, 3 * width), BF),
            head_rows, head_rows, head_rows, head_rows, flat, flat, flat,
            pltpu.VMEM((8, t), F32), pltpu.VMEM((width, t), F32), pltpu.VMEM((3 * width, t), BF),
            pltpu.VMEM((heads, BLK, HEAD_DIM), F32), pltpu.VMEM((heads, BLK, HEAD_DIM), F32),
            pltpu.VMEM((d, 3 * width), BF), pltpu.SemaphoreType.DMA((5,)), pltpu.SemaphoreType.DMA(()),
        ],
        compiler_params=pltpu.CompilerParams(vmem_limit_bytes=VMEM_LIMIT),
        cost_estimate=cost(55),
        name="attention_backward",
    )(scal, *xparts, *wparts, *daparts, a_saved, bias, segk, segq, lse)


EPSILON = 1e-05
SUB = 640


def normal_rows(hidden):
    centre = hidden - jnp.mean(hidden, axis=-1, keepdims=True)
    inverse = lax.rsqrt(jnp.mean(centre * centre, axis=-1, keepdims=True) + EPSILON)
    return centre * inverse, inverse


def norm_back(upstream, normal, inverse, gain_row):
    scaled = upstream * gain_row
    return inverse * (scaled - jnp.mean(scaled, axis=-1, keepdims=True) - normal * jnp.mean(scaled * normal, axis=-1, keepdims=True))


def gelu_share(u):
    return 0.5 * (1.0 + lax.erf(u * (1.0 / math.sqrt(2.0))))


PAD = 256


def start_weights(scal, parts, specs, wo, w1, w2, sems):
    rows, units = parts[0].shape[1], w1.shape[2]
    by_block = [[] for _ in range(5)]
    for part, (chunk, first, count) in zip(parts, specs):
        at = pl.ds(pl.multiple_of(scal[4 + chunk] * rows, rows), rows)
        for z in range(first, first + count):
            src = part.at[z - first]
            by_block[0].append(pltpu.make_async_copy(src.at[:, 2 * units:], wo.at[z, at], sems.at[0]))
            by_block[1 + z].append(pltpu.make_async_copy(src.at[:, :units], w1.at[z, at], sems.at[1 + z]))
            by_block[1 + z].append(pltpu.make_async_copy(src.at[:, units:2 * units], w2.at[z, at], sems.at[1 + z]))
    for copies in by_block:
        for copy in copies:
            copy.start()
    return by_block


def wait_all(copies):
    for copy in copies:
        copy.wait()


def post_fwd_kernel(specs, last, *refs):
    scal = refs[0]
    a, (hidden, vec, ub) = refs[1:5], refs[5:8]
    parts, rest = refs[8:8 + len(specs)], refs[8 + len(specs):]
    outs, (wo, w1, w2, xn2, sems) = rest[:-5], rest[-5:]
    h1, h2 = outs[:2]
    loads = start_weights(scal, parts, specs, wo, w1, w2, sems)
    wait_all(loads[0])
    width = a[0].shape[1]
    total = hidden[...] + vec[4:5, :]
    for i in range(4):
        total += dot_nt(a[i][...], wo[scal[i], :, :width])
    h1[...] = total
    normal, _ = normal_rows(total)
    xn2[...] = (normal * vec[2:3, :] + vec[3:4, :]).astype(BF)
    h2[...] = total + vec[5:6, :]
    units = w1.shape[2]
    for z in range(4):
        wait_all(loads[1 + z])

        def step(j, carry):
            at = pl.ds(pl.multiple_of(j * SUB, SUB), SUB)
            u = dot_nn(xn2[...], w1[z, :, at]) + ub[z, :, at]
            g = (u * gelu_share(u)).astype(BF)
            h2[...] += dot_nt(g, w2[z, :, at])
            return carry

        lax.fori_loop(0, units // SUB, step, 0)
    if not last:
        normal, _ = normal_rows(h2[...])
        outs[2][...] = (normal * vec[8:9, :] + vec[9:10, :]).astype(BF)


def post_fwd(scal, a, hidden, vec, ub, parts, specs, last):
    rows, d = hidden.shape
    units = ub.shape[2]
    anyspec = pl.BlockSpec(memory_space=pl.ANY)
    v = pl.BlockSpec(memory_space=pltpu.VMEM)
    out = [jax.ShapeDtypeStruct((rows, d), F32)] * 2 + ([] if last else [jax.ShapeDtypeStruct((rows, d), BF)])
    return pl.pallas_call(
        functools.partial(post_fwd_kernel, specs, last),
        out_shape=out,
        in_specs=[pl.BlockSpec(memory_space=pltpu.SMEM)] + [v] * 7 + [anyspec] * len(parts),
        out_specs=[v] * len(out),
        scratch_shapes=[
            pltpu.VMEM((4, d, PAD), BF), pltpu.VMEM((4, d, units), BF), pltpu.VMEM((4, d, units), BF),
            pltpu.VMEM((rows, d), BF), pltpu.SemaphoreType.DMA((5,)),
        ],
        compiler_params=pltpu.CompilerParams(vmem_limit_bytes=VMEM_LIMIT),
        cost_estimate=cost(16),
        name="rows_forward",
    )(scal, *a, hidden, vec, ub, *parts)


def post_bwd_kernel(specs, groups, *refs):
    scal = refs[0]
    a, (h1, gy, vec, ub) = refs[1:5], refs[5:9]
    parts, rest = refs[9:9 + len(specs)], refs[9 + len(specs):]
    gy1, dub, dvec = rest[:3]
    da_out = rest[3:7]
    outs = rest[7:7 + len(groups)]
    wo, w1, w2, dwo, dw1, dw2, xn2, df, xn2t, dft, dxn2, sems, osem = rest[7 + len(groups):]
    loads = start_weights(scal, parts, specs, wo, w1, w2, sems)
    rows_d = parts[0].shape[1]
    width = a[0].shape[1]
    places = []
    for out, chunks in zip(outs, groups):
        for i, chunk in enumerate(chunks):
            places.append((out.at[i], pl.ds(pl.multiple_of(scal[4 + chunk] * rows_d, rows_d), rows_d)))
    normal, inverse = normal_rows(h1[...])
    xlow = (normal * vec[2:3, :] + vec[3:4, :]).astype(BF)
    xn2[...] = xlow
    xn2t[...] = xlow.T
    low = gy[...].astype(BF)
    df[...] = low
    dft[...] = low.T
    dvec[...] = jnp.zeros_like(dvec)
    dvec[5:6, :] = jnp.sum(low.astype(F32), axis=0, keepdims=True)
    dxn2[...] = jnp.zeros_like(dxn2)
    units = w1.shape[2]
    stores = []
    for z in range(4):
        wait_all(loads[1 + z])

        def step(j, carry):
            at = pl.ds(pl.multiple_of(j * SUB, SUB), SUB)
            u = dot_nn(xn2[...], w1[z, :, at]) + ub[z, :, at]
            share = gelu_share(u)
            g = (u * share).astype(BF)
            dg = dot_nn(df[...], w2[z, :, at])
            slope = share + u * jnp.exp(-0.5 * u * u) * (1.0 / math.sqrt(2.0 * math.pi))
            du = (dg * slope).astype(BF)
            dub[z, :, at] = jnp.sum(du.astype(F32), axis=0, keepdims=True)
            dw1[z, :, at] = dot_nn(xn2t[...], du).astype(BF)
            dw2[z, :, at] = dot_nn(dft[...], g).astype(BF)
            dxn2[...] += dot_nt(du, w1[z, :, at])
            return carry

        lax.fori_loop(0, units // SUB, step, 0)
        for out, at in places:
            for i, src in enumerate((dw1, dw2)):
                stores.append(pltpu.make_async_copy(src.at[z, at], out.at[z, :, i * units:(i + 1) * units], osem))
                stores[-1].start()
    wait_all(loads[0])
    upstream = dxn2[...]
    dvec[2:3, :] = jnp.sum(upstream * normal, axis=0, keepdims=True)
    dvec[3:4, :] = jnp.sum(upstream, axis=0, keepdims=True)
    total = gy[...] + norm_back(upstream, normal, inverse, vec[2:3, :])
    gy1[...] = total
    low = total.astype(BF)
    dvec[4:5, :] = jnp.sum(low.astype(F32), axis=0, keepdims=True)
    dat = low.T
    dwo[...] = jnp.zeros_like(dwo)
    for i in range(4):
        slot = scal[i]
        dwo[slot, :, :width] = dot_nn(dat, a[i][...]).astype(BF)
        da_out[i][...] = dot_nn(low, wo[slot, :, :width]).astype(BF)
    for out, at in places:
        for z in range(4):
            stores.append(pltpu.make_async_copy(dwo.at[z, at], out.at[z, :, 2 * units:], osem))
            stores[-1].start()
    wait_all(stores)


def post_bwd(scal, a, h1, gy, vec, ub, parts, specs, groups):
    rows, d = h1.shape
    rows_d, width, units = parts[0].shape[1], a[0].shape[1], ub.shape[2]
    anyspec = pl.BlockSpec(memory_space=pl.ANY)
    v = pl.BlockSpec(memory_space=pltpu.VMEM)
    out = [jax.ShapeDtypeStruct((rows, d), F32), jax.ShapeDtypeStruct((4, 1, units), F32), jax.ShapeDtypeStruct((8, d), F32)]
    out += [jax.ShapeDtypeStruct((rows, width), BF)] * 4
    out += [jax.ShapeDtypeStruct((len(chunks), 4, rows_d, 2 * units + PAD), BF) for chunks in groups]
    matrix = pltpu.VMEM((4, d, units), BF)
    thin = pltpu.VMEM((4, d, PAD), BF)
    return pl.pallas_call(
        functools.partial(post_bwd_kernel, specs, groups),
        out_shape=out,
        in_specs=[pl.BlockSpec(memory_space=pltpu.SMEM)] + [v] * 8 + [anyspec] * len(parts),
        out_specs=[v] * 7 + [anyspec] * len(groups),
        scratch_shapes=[
            thin, matrix, matrix, thin, matrix, matrix,
            pltpu.VMEM((rows, d), BF), pltpu.VMEM((rows, d), BF), pltpu.VMEM((d, rows), BF), pltpu.VMEM((d, rows), BF),
            pltpu.VMEM((rows, d), F32), pltpu.SemaphoreType.DMA((5,)), pltpu.SemaphoreType.DMA(()),
        ],
        compiler_params=pltpu.CompilerParams(vmem_limit_bytes=VMEM_LIMIT),
        cost_estimate=cost(33),
        name="rows_backward",
    )(scal, *a, h1, gy, vec, ub, *parts)


MOMENTUM = 0.9
AVERAGE_KEEP = 0.9
WEIGHT_DECAY = 0.0001
RATE_SCALE = 0.02
ROWS_AXES = ("y", "x", "c")
COLS_AXES = ("h", "b")
EVERY = ROWS_AXES + COLS_AXES


def swap(value, name):
    return lax.ppermute(value, name, [(0, 1), (1, 0)])


def home(value):
    return lax.ppermute(value, ("c", "h"), [(0, 0), (1, 2), (2, 1), (3, 3)])


def corner(value):
    return lax.ppermute(value, ("c", "b"), [(0, 3), (1, 2), (2, 1), (3, 0)])


def double(value, name):
    return jnp.concatenate([value, swap(value, name)], axis=0)


def f32(value):
    return value.astype(F32)


def after(value, *others):
    return lax.optimization_barrier((value,) + others)[0]


def reduce_plane(keep, rest, for_x, for_y):
    def pair(chunk, half):
        return f32(keep[chunk, half]) + f32(rest[chunk, half])

    whole = slice(0, 4)
    to_x = pair(1, whole) + jnp.pad(f32(for_x), ((2, 0), (0, 0), (0, 0)))
    to_y = pair(2, whole) + jnp.pad(f32(for_y), ((0, 2), (0, 0), (0, 0)))
    return (lambda: pair(0, whole)), swap(to_x.astype(BF), "x"), swap(to_y.astype(BF), "y")


def reduce_h(total):
    return total[0] + f32(swap(total[1].astype(BF), "h"))


def scatter(value):
    value = lax.psum_scatter(f32(value), COLS_AXES, scatter_dimension=0, tiled=True)[0]
    return lax.psum_scatter(value, ROWS_AXES, scatter_dimension=0, tiled=True)


def sgd_step(weight, gradient, moment, average, step_rate):
    decayed = gradient + WEIGHT_DECAY * weight
    moment_next = MOMENTUM * moment + decayed
    weight_next = weight - step_rate * (decayed + MOMENTUM * moment_next)
    average_next = AVERAGE_KEEP * average + (1.0 - AVERAGE_KEEP) * weight_next
    return (weight_next, moment_next, average_next)


def local(
    tokens_in, cotangent, lengths, segments, bucket_map, bucket_tokens,
    attention, feedforward, vectors, head_bias, unit_bias,
    attention_moment, feedforward_moment, vectors_moment, head_moment, unit_moment,
    attention_mean, feedforward_mean, vectors_mean, head_mean, unit_mean,
):
    rows, width_d = tokens_in.shape
    layer_count = attention.shape[0]
    iy, ix, ic, ih, ib = (lax.axis_index(name) for name in EVERY)
    x_size = lax.axis_size("x")
    fast = lax.axis_size("y") == 2 and x_size == 2
    dp_size = lax.axis_size("y") * x_size * 2
    dp_place = (iy * x_size + ix) * 2 + ic
    mp_place = 2 * ih + ib
    quarter = 2 * ic + ib
    stays = ic == ih
    pack_length = rows * 4
    nb = pack_length // BLK

    low_attention, low_feedforward, low_vectors, low_head, low_unit = lax.optimization_barrier(
        tuple(p.astype(BF) for p in (attention, feedforward, vectors, head_bias, unit_bias))
    )
    head_width, units = attention.shape[3], feedforward.shape[3]
    qkv_low = jnp.concatenate([low_attention[:, i] for i in range(3)], axis=2)
    rows_w = attention.shape[2]
    spare_width = units // rows_w if fast else 0
    spare = jnp.zeros((layer_count, rows_w, PAD - head_width - spare_width), BF)
    if fast:
        spare = jnp.concatenate([low_unit.reshape(layer_count, rows_w, spare_width), spare], axis=2)
    ff_low = [
        jnp.concatenate([low_feedforward[layer, 0], low_feedforward[layer, 1],
                         low_attention[layer, 3], spare[layer]], axis=1)
        for layer in range(layer_count)
    ]

    hidden_low = home(tokens_in)
    meta = jnp.concatenate([segments[0], jnp.sum(lengths[0])[None], bucket_map])
    meta = jnp.where(stays, meta, swap(meta, "c"))
    segment_row, total_live, bucket = meta[:pack_length], meta[pack_length], meta[pack_length + 1]

    if fast:
        v8 = double(double(double(low_vectors.reshape(1, layer_count * 6, -1), "c"), "x"), "y")
        v8 = v8.reshape(2, 2, 2, layer_count * 6, -1)
        for axis, place in ((0, iy), (1, ix), (2, ic)):
            v8 = jnp.where(place == 1, jnp.flip(v8, axis), v8)
        full_vectors = v8.reshape(8, layer_count * 6, -1).transpose(1, 0, 2).reshape(layer_count, 6, width_d)
        head_pad = jnp.pad(low_head, ((0, 0), (0, 14), (0, 2 * head_width)))
        packed = jnp.concatenate([qkv_low, head_pad], axis=1)
        far = swap(packed, "h")
        mine, theirs = jnp.where(stays, packed, far), jnp.where(stays, far, packed)
        heads_used = mine[:, rows_w:rows_w + 2, :head_width]
        both_cores = jnp.stack([mine[:, :rows_w], swap(theirs[:, :rows_w], "c")])
        across = swap(both_cores, "x")
        qkv_parts = [both_cores, across, swap(both_cores, "y"), swap(across, "y")]
        chunk_places = [dp_place ^ (2 * (p % 4) + p // 4) for p in range(8)]
        turned = [2 * (i % 2) + i // 2 for i in range(4)]
        slots = jnp.stack([jnp.where(stays, turned[i], turned[i ^ 2]) for i in range(4)])
        specs = [(0, 0, 4), (1, 0, 4), (2, 0, 4), (3, 0, 2), (3, 2, 2)]
        specs = tuple(specs + [(chunk + 4, first, count) for chunk, first, count in specs])
        groups = ((0, 1, 2, 3), (7,), (4, 5, 6))
    else:
        full_vectors = lax.all_gather(low_vectors, ROWS_AXES, axis=2, tiled=True)
        units4 = lax.all_gather(low_unit, COLS_AXES, axis=0)
        heads_used = lax.all_gather(low_head, COLS_AXES, axis=0)[quarter]
        qkv_parts = [lax.all_gather(lax.all_gather(qkv_low, ROWS_AXES, axis=1, tiled=True), COLS_AXES, axis=0)[quarter][None]]
        whole_ff = [lax.all_gather(lax.all_gather(w, ROWS_AXES, axis=0, tiled=True), COLS_AXES, axis=0) for w in ff_low]
        chunk_places = [jnp.int32(0)]
        slots = jnp.stack([quarter ^ i for i in range(4)])
        specs = ((0, 0, 4),)
        groups = ((0,),)
    vec = f32(full_vectors)
    head_rows = f32(heads_used)

    positions = jnp.arange(pack_length, dtype=jnp.int32)
    own_segment = jnp.where(positions < total_live, segment_row, 64 + positions)
    by_block = own_segment.reshape(nb, BLK)
    first_block = jnp.sum(own_segment[None, :] < by_block[:, :1], axis=1) // BLK
    end_block = (jnp.sum(own_segment[None, :] <= by_block[:, -1:], axis=1) + BLK - 1) // BLK
    places = jnp.stack([quarter ^ rel for rel in range(4)])
    chunk_array = jnp.stack(chunk_places).astype(jnp.int32)
    scal = jnp.concatenate([first_block, end_block, places, jnp.zeros((1,), jnp.int32), chunk_array]).astype(jnp.int32)
    scal_rows = jnp.concatenate([slots.astype(jnp.int32), chunk_array])
    segk, segq = own_segment[:, None], own_segment[None, :]
    live_own = (quarter * rows + jnp.arange(rows) < total_live)[:, None]
    counts_float = f32(bucket_tokens)
    chosen = jnp.arange(bucket_tokens.shape[0]) == bucket
    pack_weight = bucket_tokens.shape[0] * jnp.sum(jnp.where(chosen, counts_float, 0.0)) / jnp.sum(counts_float)

    def vec_rows(layer, other):
        return jnp.concatenate([vec[layer], jnp.zeros((2, width_d), F32), vec[other], jnp.zeros((2, width_d), F32)])

    hidden = f32(hidden_low)
    normal, _ = normal_rows(hidden)
    normed = (normal * vec[0, 0] + vec[0, 1]).astype(BF)
    saved = []
    if fast:
        line = double(double(ff_low[0][None], "h"), "b")
        x_part, y_part = swap(line, "x"), swap(line, "y")
    for layer in range(layer_count):
        last = layer == layer_count - 1
        over = swap(normed, "b")
        normed_parts = [normed, over, swap(normed, "c"), swap(over, "c")]
        if fast:
            if layer:
                normed_parts, x_part, y_part = lax.optimization_barrier((normed_parts, x_part, y_part))
            if not last:
                ahead = after(ff_low[layer + 1][None], *normed_parts)
                ahead_h = swap(ahead, "h")
            own_parts = [line, x_part, y_part]
            if layer:
                own_parts += [swap(y_part[:2], "x"), swap(x_part[2:], "y")]
        mixed, log_total = attn_fwd(scal, normed_parts, qkv_parts, layer, head_rows[layer], segk, segq)
        if fast:
            if not last:
                mixed, ahead_h = lax.optimization_barrier((mixed, ahead_h))
            if layer:
                mixed, own_parts = lax.optimization_barrier((mixed, own_parts))
            else:
                mixed, x_part, y_part = lax.optimization_barrier((mixed, x_part, y_part))
                own_parts = [line, x_part, y_part, swap(y_part[:2], "x"), swap(x_part[2:], "y")]
        own_mixed = [mixed[0], swap(mixed[1], "b"), swap(mixed[2], "c"), corner(mixed[3])]
        vec16 = vec_rows(layer, 0 if last else layer + 1)
        if fast:
            at = 2 * units + head_width
            unit_row = f32(line[:, :, at:at + spare_width].reshape(4, 1, units))
            parts = own_parts + [swap(part, "c") for part in own_parts]
            if not last:
                ahead = jnp.concatenate([ahead, ahead_h])
                ahead_b = swap(after(ahead, *own_mixed), "b")
                own_mixed, ahead_b = lax.optimization_barrier((own_mixed, ahead_b))
                line = jnp.concatenate([ahead, ahead_b])
                x_part, y_part = swap(line, "x"), swap(line, "y")
        else:
            parts = [whole_ff[layer]]
            unit_row = f32(units4[:, layer][:, None, :])
        outs = post_fwd(scal_rows, own_mixed, hidden, vec16, unit_row, parts, specs, last)
        saved.append((hidden, normed_parts, mixed, log_total, own_mixed, outs[0], unit_row, vec16, parts))
        hidden = outs[1]
        if not last:
            normed = outs[2]
    hidden_out = f32(home(jnp.where(live_own, hidden, 0.0).astype(BF)))
    hidden_out = jnp.where(stays, jnp.where(live_own, hidden, 0.0), hidden_out)

    cotangent_here = home(after(cotangent, saved[0][5]))
    upstream = jnp.where(live_own, f32(cotangent_here) * pack_weight, 0.0)
    qkv_grads, matrix_grads, vector_grads, head_grads, unit_grads = [], [], [], [], []
    waiting = None
    for layer in reversed(range(layer_count)):
        hidden, normed_parts, mixed, log_total, own_mixed, middle, unit_row, vec16, parts = saved[layer]
        outs = post_bwd(scal_rows, own_mixed, middle, upstream, vec16, unit_row, parts, specs, groups)
        if waiting is not None:
            outs, beside = lax.optimization_barrier((outs, waiting[1:]))
            own = waiting[0]() + f32(beside[0]) + f32(beside[1])
        upstream, d_unit, d_vec = outs[:3]
        d_mixed, terms = outs[3:7], outs[7:]
        d_parts = [d_mixed[0], swap(d_mixed[1], "b"), swap(d_mixed[2], "c"), corner(d_mixed[3])]
        if fast:
            keep, send_far, send = terms
            far_sum = (f32(keep[3]) + f32(swap(send_far, "c")[0])).astype(BF)
            rest = swap(after(send, *d_parts), "c")
            for_x, for_y = swap(far_sum[2:], "y"), swap(far_sum[:2], "x")
            if waiting is not None:
                to_b = swap(after(own[2:].astype(BF), *d_parts), "b")
        outs = attn_bwd(scal, normed_parts, qkv_parts, layer, d_parts, mixed, head_rows[layer], segk, segq, log_total)
        if fast:
            outs, rest, for_x, for_y = lax.optimization_barrier((outs, rest, for_x, for_y))
            if waiting is not None:
                outs, to_b = lax.optimization_barrier((outs, to_b))
                matrix_grads.append(reduce_h(own[:2] + f32(to_b)))
            waiting = reduce_plane(keep, rest, for_x, for_y)
        else:
            matrix_grads.append(scatter(terms[0][0]))
        d_rows, d_head = outs[:2]
        qkv_grads.append(outs[2:])
        got = swap(d_rows[2:4], "c")
        got2 = swap((f32(d_rows[1]) + f32(got[1])).astype(BF), "b")
        d_normed = f32(d_rows[0]) + f32(got[0]) + f32(got2)
        normal, inverse = normal_rows(hidden)
        upstream = upstream + norm_back(d_normed, normal, inverse, vec[layer, 0])
        vector_grads.append(jnp.concatenate([
            jnp.sum(d_normed * normal, axis=0)[None], jnp.sum(d_normed, axis=0)[None], d_vec[2:6]]))
        head_grads.append(d_head)
        unit_grads.append(d_unit[:, 0])
    vector_sum = jnp.stack(vector_grads[::-1])
    head_sum = jnp.stack(head_grads[::-1])
    unit_sum = jnp.stack(unit_grads[::-1], axis=1)
    v_size, u_size = vector_sum.size, unit_sum.size // 4
    if fast:
        by_core = [jnp.stack([grads[core] for grads in qkv_grads[::-1]]) for core in range(2)]
        other = swap(by_core[1], "c")
        near = f32(jnp.where(stays, by_core[0], other))
        far = jnp.where(stays, other, by_core[0])
        both = near + f32(swap(far, "h"))
        flat_v, flat_e = vector_sum.reshape(-1), head_sum.reshape(-1)
        flat_u = unit_sum.reshape(4, -1)
        near_e = jnp.where(stays, flat_e, 0.0)
        got = swap(jnp.concatenate([flat_v, flat_u[1], flat_u[3], flat_e - near_e]), "h")
        flat = jnp.concatenate([flat_v, flat_u[0], flat_u[2], near_e]) + got
        flat = flat + swap(flat, "c")
        both, flat, beside = lax.optimization_barrier((both, flat, waiting[1:]))
        own = waiting[0]() + f32(beside[0]) + f32(beside[1])
        to_b = swap(own[2:].astype(BF), "b")
        got = swap(both[:, 1::2].astype(BF), "x")
        flat = flat + swap(flat, "x")
        to_b, got, flat = lax.optimization_barrier((to_b, got, flat))
        own = own[:2] + f32(to_b)
        to_h = swap(own[1].astype(BF), "h")
        got2 = swap((both[:, 2] + f32(got[:, 1])).astype(BF), "y")
        qkv_gradient = both[:, 0] + f32(got[:, 0]) + f32(got2)
        flat = flat + swap(flat, "y")
        sent = swap(jnp.concatenate([flat[:v_size], flat[v_size + u_size:v_size + 2 * u_size]]), "b")
        vector_total = (flat[:v_size] + sent[:v_size]).reshape(vector_sum.shape)
        unit_gradient = (flat[v_size:v_size + u_size] + sent[v_size:]).reshape(unit_bias.shape)
        flat_e = flat[v_size + 2 * u_size:]
        head_gradient = flat_e.reshape(head_bias.shape)
        matrix_grads.append(own[0] + f32(to_h))
    else:
        empty = jnp.zeros((4,) + qkv_grads[0][0].shape[1:], F32)
        qkv_gradient = jnp.stack([scatter(empty.at[quarter].set(f32(grads[0][0]))) for grads in qkv_grads[::-1]])
    matrix_gradient = jnp.stack(matrix_grads[::-1])
    attention_gradient = jnp.stack(
        [qkv_gradient[:, :, i * head_width:(i + 1) * head_width] for i in range(3)]
        + [matrix_gradient[:, :, 2 * units:2 * units + head_width]], axis=1)
    feedforward_gradient = jnp.stack([matrix_gradient[:, :, :units], matrix_gradient[:, :, units:2 * units]], axis=1)

    if not fast:
        placed = jnp.zeros((4,) + head_sum.shape, F32).at[quarter].set(head_sum)
        vector_total, unit_total, head_total = lax.psum((vector_sum, unit_sum, placed), EVERY)
        unit_gradient, head_gradient = unit_total[mp_place], head_total[mp_place]
    chunk = width_d // dp_size
    vectors_gradient = lax.dynamic_slice_in_dim(vector_total, dp_place * chunk, chunk, 2)

    input_gradient = f32(home(upstream.astype(BF)))
    input_gradient = jnp.where(stays, upstream, input_gradient)
    step_rate = RATE_SCALE * lax.rsqrt(jnp.float32(dp_size * pack_length))
    weights = (attention, feedforward, vectors, head_bias, unit_bias)
    gradients = (attention_gradient, feedforward_gradient, vectors_gradient, head_gradient, unit_gradient)
    moments = (attention_moment, feedforward_moment, vectors_moment, head_moment, unit_moment)
    averages = (attention_mean, feedforward_mean, vectors_mean, head_mean, unit_mean)
    steps = [sgd_step(*leaf, step_rate) for leaf in zip(weights, gradients, moments, averages)]
    return (
        (hidden_out, input_gradient) + gradients + tuple(s[0] for s in steps) + tuple(s[1] for s in steps)
        + tuple(s[2] for s in steps) + (steps[0][0].astype(BF), steps[1][0].astype(BF))
    )


def solution(mesh):
    dp_size = mesh.shape["dp"]
    inner = jax.sharding.Mesh(mesh.devices.reshape(2, dp_size // 4, 2, 2, 2), EVERY)
    rows, cols = ROWS_AXES, COLS_AXES
    tokens = P(rows + cols, None)
    params = (P(None, None, rows, cols), P(None, None, rows, cols), P(None, None, rows), P(None, None, cols), P(None, cols))
    in_specs = (tokens, tokens, P(rows, None), P(rows, None), P(rows), P()) + params * 3
    out_specs = (tokens, tokens) + params * 4 + params[:2]
    return jax.shard_map(local, mesh=inner, in_specs=in_specs, out_specs=out_specs, check_vma=False)
```

```python
import functools, math
import jax, jax.numpy as jnp
from jax import lax
from jax.experimental import pallas as pl
from jax.experimental.pallas import tpu as pltpu
from jax.sharding import PartitionSpec as P

HEAD_DIM = 32
MASKED = -1e30
LOG2E = math.log2(math.e)
SCORE = HEAD_DIM ** (-0.5)
SCORE2 = SCORE * LOG2E
BLK = 256
BF = jnp.bfloat16
F32 = jnp.float32
VMEM_LIMIT = 60 * 1024 * 1024


def cost(micros):
    return pl.CostEstimate(flops=micros * 1100000000, bytes_accessed=1000000, transcendentals=0)


def dot_nn(a, b):
    return lax.dot_general(a, b, (((1,), (0,)), ((), ())), preferred_element_type=F32)


def dot_nt(a, b):
    return lax.dot_general(a, b, (((1,), (1,)), ((), ())), preferred_element_type=F32)


def load_parts(scal, parts, dest, first, rows, sem):
    copies = []
    for i, part in enumerate(parts):
        start = pl.multiple_of(scal[first + i] * rows, rows)
        copies.append(pltpu.make_async_copy(part, dest.at[pl.ds(start, rows)], sem))
    for copy in copies:
        copy.start()
    return copies


def chunks_of(wrefs, layer):
    return [w.at[core, layer] for core in range(wrefs[0].shape[0]) for w in wrefs]


def attn_fwd_kernel(nb, nw, layer, *refs):
    scal = refs[0]
    xparts = refs[1:5]
    wparts = chunks_of(refs[5:5 + nw], layer)
    bias, segk, segq, out, lse = refs[5 + nw:10 + nw]
    xs, ws, ks, qt, vt, acc, scores, sems = refs[10 + nw:]
    heads = ks.shape[0]
    width = heads * HEAD_DIM
    rows = xparts[0].shape[0]
    base = 2 * nb
    wcopies = load_parts(scal, wparts, ws, base + 5, wparts[0].shape[0], sems.at[4])
    xcopies = [load_parts(scal, [p], xs, base + i, rows, sems.at[i])[0] for i, p in enumerate(xparts)]
    for c in wcopies:
        c.wait()
    for i in range(4):
        xcopies[i].wait()
        start = pl.multiple_of(scal[base + i] * rows, rows)
        y = dot_nn(xs[pl.ds(start, rows), :], ws[...])
        qt[:, pl.ds(start, rows)] = (y[:, :width] + bias[0:1, :]).T.astype(BF)
        k = y[:, width:2 * width].astype(BF)
        for h in range(heads):
            ks[h, pl.ds(start, rows), :] = k[:, h * HEAD_DIM:(h + 1) * HEAD_DIM]
        vt[:, pl.ds(start, rows)] = (y[:, 2 * width:] + bias[1:2, :]).T.astype(BF)
    lse[...] = jnp.zeros_like(lse)
    per = rows // BLK

    def fold(z):
        return z.reshape(BLK // 8, 8, BLK)

    def q_block(qb, carry):
        q0 = pl.multiple_of(qb * BLK, BLK)
        acc[...] = jnp.zeros_like(acc)
        sq = segq[:, pl.ds(q0, BLK)]
        first, end = scal[qb], scal[nb + qb]

        def score_block(kb, ms):
            k0 = pl.multiple_of(kb * BLK, BLK)
            mask = segk[pl.ds(k0, BLK), :] == sq
            new = []
            for h in range(heads):
                hs = slice(h * HEAD_DIM, (h + 1) * HEAD_DIM)
                s = dot_nn(ks[h, pl.ds(k0, BLK), :], qt[hs, pl.ds(q0, BLK)])
                s = jnp.where(mask, s, MASKED)
                scores[h, kb] = s
                new.append(jnp.maximum(ms[h], jnp.max(fold(s), axis=0)))
            return tuple(new)

        ms = lax.fori_loop(first, end, score_block, (jnp.full((8, BLK), MASKED, F32),) * heads)
        tops = [jnp.max(m, axis=0, keepdims=True) * SCORE2 for m in ms]

        def mix_block(kb, ls):
            k0 = pl.multiple_of(kb * BLK, BLK)
            new = []
            for h in range(heads):
                hs = slice(h * HEAD_DIM, (h + 1) * HEAD_DIM)
                p = jnp.exp2(scores[h, kb] * SCORE2 - tops[h])
                acc[hs, :] += dot_nn(vt[hs, pl.ds(k0, BLK)], p.astype(BF))
                new.append(ls[h] + jnp.sum(fold(p), axis=0))
            return tuple(new)

        ls = lax.fori_loop(first, end, mix_block, (jnp.zeros((8, BLK), F32),) * heads)
        for h in range(heads):
            hs = slice(h * HEAD_DIM, (h + 1) * HEAD_DIM)
            l = jnp.sum(ls[h], axis=0, keepdims=True)
            acc[hs, :] = acc[hs, :] * (1.0 / l)
            lse[h:h + 1, pl.ds(q0, BLK)] = tops[h] + jnp.log2(l)
        part = lax.bitwise_xor(lax.div(qb, per), scal[base])
        out[part, pl.ds(pl.multiple_of(lax.rem(qb, per) * BLK, BLK), BLK), :] = acc[...].T.astype(BF)
        return carry

    lax.fori_loop(0, nb, q_block, 0)


def attn_fwd(scal, xparts, wparts, layer, bias, segk, segq):
    rows, d = xparts[0].shape
    t = 4 * rows
    width = wparts[0].shape[3] // 3
    heads = width // HEAD_DIM
    nb = t // BLK
    npc = len(wparts)
    anyspec = pl.BlockSpec(memory_space=pl.ANY)
    v = pl.BlockSpec(memory_space=pltpu.VMEM)
    return pl.pallas_call(
        functools.partial(attn_fwd_kernel, nb, npc, layer),
        out_shape=(jax.ShapeDtypeStruct((4, rows, width), BF), jax.ShapeDtypeStruct((8, t), F32)),
        in_specs=[pl.BlockSpec(memory_space=pltpu.SMEM)] + [anyspec] * (4 + npc) + [v] * 3,
        out_specs=(v, v),
        scratch_shapes=[
            pltpu.VMEM((t, d), BF), pltpu.VMEM((d, 3 * width), BF), pltpu.VMEM((heads, t, HEAD_DIM), BF),
            pltpu.VMEM((width, t), BF), pltpu.VMEM((width, t), BF), pltpu.VMEM((width, BLK), F32),
            pltpu.VMEM((heads, nb, BLK, BLK), F32),
            pltpu.SemaphoreType.DMA((5,)),
        ],
        compiler_params=pltpu.CompilerParams(vmem_limit_bytes=VMEM_LIMIT),
        cost_estimate=cost(28),
        name="attention_forward",
    )(scal, *xparts, *wparts, bias, segk, segq)


def attn_bwd_kernel(nb, nw, layer, *refs):
    scal = refs[0]
    xparts = refs[1:5]
    groups = refs[5].shape[0]
    wparts = chunks_of(refs[5:5 + nw], layer)
    npc = len(wparts)
    daparts = refs[5 + nw:9 + nw]
    a_saved, bias, segk, segq, lse, dx, dbias = refs[9 + nw:16 + nw]
    dw_out = refs[16 + nw:16 + nw + groups]
    xs, ws, qs, ks, vs, das, qt, kt, dat, delta, dqt, dall, dka, dva, dw, sems, osem = refs[16 + nw + groups:]
    heads = ks.shape[0]
    width = heads * HEAD_DIM
    rows = xparts[0].shape[0]
    base = 2 * nb
    wcopies = load_parts(scal, wparts, ws, base + 5, wparts[0].shape[0], sems.at[4])
    xcopies = [load_parts(scal, [p], xs, base + i, rows, sems.at[i])[0] for i, p in enumerate(xparts)]
    for c in wcopies:
        c.wait()
    for i in range(4):
        xcopies[i].wait()
        start = pl.multiple_of(scal[base + i] * rows, rows)
        at = pl.ds(start, rows)
        x = xs[at, :]
        y = dot_nn(x, ws[...])
        q = y[:, :width] + bias[0:1, :]
        qt[:, at] = q.T.astype(BF)
        ql = q.astype(BF)
        kf = y[:, width:2 * width]
        kt[:, at] = kf.T.astype(BF)
        kl = kf.astype(BF)
        vl = (y[:, 2 * width:] + bias[1:2, :]).astype(BF)
        dal = daparts[i][...]
        daf = dal.astype(F32).T
        dat[:, at] = daf.astype(BF)
        prod = daf * a_saved[i].astype(F32).T
        for h in range(heads):
            hs = slice(h * HEAD_DIM, (h + 1) * HEAD_DIM)
            qs[h, at, :] = ql[:, hs]
            ks[h, at, :] = kl[:, hs]
            vs[h, at, :] = vl[:, hs]
            das[h, at, :] = dal[:, hs]
            delta[h:h + 1, at] = jnp.sum(prod[hs, :], axis=0, keepdims=True)
    dqt[...] = jnp.zeros_like(dqt)

    def k_block(kb, carry):
        k0 = pl.multiple_of(kb * BLK, BLK)
        kat = pl.ds(k0, BLK)
        dka[...] = jnp.zeros_like(dka)
        dva[...] = jnp.zeros_like(dva)
        sk = segk[kat, :]

        def q_block(qb, c2):
            q0 = pl.multiple_of(qb * BLK, BLK)
            qat = pl.ds(q0, BLK)
            mask = sk == segq[:, qat]
            for h in range(heads):
                hs = slice(h * HEAD_DIM, (h + 1) * HEAD_DIM)
                s = dot_nn(ks[h, kat, :], qt[hs, qat])
                p = jnp.where(mask, jnp.exp2(s * SCORE2 - lse[h:h + 1, qat]), 0.0)
                dp = dot_nn(vs[h, kat, :], dat[hs, qat])
                dva[h] += dot_nn(p.astype(BF), das[h, qat, :])
                ds = (p * (dp - delta[h:h + 1, qat])).astype(BF)
                dka[h] += dot_nn(ds, qs[h, qat, :])
                dqt[hs, qat] += dot_nn(kt[hs, kat], ds)
            return c2

        lax.fori_loop(scal[kb], scal[nb + kb], q_block, 0)
        for h in range(heads):
            hs = slice(h * HEAD_DIM, (h + 1) * HEAD_DIM)
            dall[width + h * HEAD_DIM:width + (h + 1) * HEAD_DIM, kat] = (dka[h].T * SCORE).astype(BF)
            dall[2 * width + h * HEAD_DIM:2 * width + (h + 1) * HEAD_DIM, kat] = dva[h].T.astype(BF)
        return carry

    lax.fori_loop(0, nb, k_block, 0)
    dall[:width, :] = (dqt[...] * SCORE).astype(BF)
    dbias[0:1, :] = jnp.sum(dall[:width, :].astype(F32), axis=1)[None, :]
    dbias[1:2, :] = jnp.sum(dall[2 * width:, :].astype(F32), axis=1)[None, :]
    dw[...] = dot_nn(dall[...], xs[...]).T.astype(dw.dtype)
    rows_d, per = wparts[0].shape[0], npc // groups
    stores = []
    for p in range(npc):
        at = pl.ds(pl.multiple_of(scal[base + 5 + p] * rows_d, rows_d), rows_d)
        stores.append(pltpu.make_async_copy(dw.at[at], dw_out[p // per].at[p % per], osem))
        stores[-1].start()
    for i in range(4):
        start = pl.multiple_of(scal[base + i] * rows, rows)
        at = pl.ds(start, rows)
        dx[i] = dot_nt(dall[:, at].astype(F32).T.astype(BF), ws[...]).astype(BF)
    for copy in stores:
        copy.wait()


def attn_bwd(scal, xparts, wparts, layer, daparts, a_saved, bias, segk, segq, lse):
    rows, d = xparts[0].shape
    t = 4 * rows
    groups, _, rows_w, width = wparts[0].shape
    width //= 3
    heads = width // HEAD_DIM
    nb = t // BLK
    npc = len(wparts)
    anyspec = pl.BlockSpec(memory_space=pl.ANY)
    v = pl.BlockSpec(memory_space=pltpu.VMEM)
    head_rows = pltpu.VMEM((heads, t, HEAD_DIM), BF)
    flat = pltpu.VMEM((width, t), BF)
    return pl.pallas_call(
        functools.partial(attn_bwd_kernel, nb, npc, layer),
        out_shape=(
            jax.ShapeDtypeStruct((4, rows, d), BF),
            jax.ShapeDtypeStruct((2, width), F32),
        ) + (jax.ShapeDtypeStruct((npc, rows_w, 3 * width), BF),) * groups,
        in_specs=[pl.BlockSpec(memory_space=pltpu.SMEM)] + [anyspec] * (4 + npc) + [v] * 9,
        out_specs=(v, v) + (anyspec,) * groups,
        scratch_shapes=[
            pltpu.VMEM((t, d), BF), pltpu.VMEM((d, 3 * width), BF),
            head_rows, head_rows, head_rows, head_rows, flat, flat, flat,
            pltpu.VMEM((8, t), F32), pltpu.VMEM((width, t), F32), pltpu.VMEM((3 * width, t), BF),
            pltpu.VMEM((heads, BLK, HEAD_DIM), F32), pltpu.VMEM((heads, BLK, HEAD_DIM), F32),
            pltpu.VMEM((d, 3 * width), BF), pltpu.SemaphoreType.DMA((5,)), pltpu.SemaphoreType.DMA(()),
        ],
        compiler_params=pltpu.CompilerParams(vmem_limit_bytes=VMEM_LIMIT),
        cost_estimate=cost(55),
        name="attention_backward",
    )(scal, *xparts, *wparts, *daparts, a_saved, bias, segk, segq, lse)


EPSILON = 1e-05
SUB = 640


def normal_rows(hidden):
    centre = hidden - jnp.mean(hidden, axis=-1, keepdims=True)
    inverse = lax.rsqrt(jnp.mean(centre * centre, axis=-1, keepdims=True) + EPSILON)
    return centre * inverse, inverse


def norm_back(upstream, normal, inverse, gain_row):
    scaled = upstream * gain_row
    return inverse * (scaled - jnp.mean(scaled, axis=-1, keepdims=True) - normal * jnp.mean(scaled * normal, axis=-1, keepdims=True))


def gelu_share(u):
    return 0.5 * (1.0 + lax.erf(u * (1.0 / math.sqrt(2.0))))


PAD = 256


def start_weights(scal, parts, specs, wo, w1, w2, sems):
    rows, units = parts[0].shape[1], w1.shape[2]
    by_block = [[] for _ in range(5)]
    for part, (chunk, first, count) in zip(parts, specs):
        at = pl.ds(pl.multiple_of(scal[4 + chunk] * rows, rows), rows)
        for z in range(first, first + count):
            src = part.at[z - first]
            by_block[0].append(pltpu.make_async_copy(src.at[:, 2 * units:], wo.at[z, at], sems.at[0]))
            by_block[1 + z].append(pltpu.make_async_copy(src.at[:, :units], w1.at[z, at], sems.at[1 + z]))
            by_block[1 + z].append(pltpu.make_async_copy(src.at[:, units:2 * units], w2.at[z, at], sems.at[1 + z]))
    for copies in by_block:
        for copy in copies:
            copy.start()
    return by_block


def wait_all(copies):
    for copy in copies:
        copy.wait()


def post_fwd_kernel(specs, last, *refs):
    scal = refs[0]
    a, (hidden, vec, ub) = refs[1:5], refs[5:8]
    parts, rest = refs[8:8 + len(specs)], refs[8 + len(specs):]
    outs, (wo, w1, w2, xn2, sems) = rest[:-5], rest[-5:]
    h1, h2 = outs[:2]
    loads = start_weights(scal, parts, specs, wo, w1, w2, sems)
    wait_all(loads[0])
    width = a[0].shape[1]
    total = hidden[...] + vec[4:5, :]
    for i in range(4):
        total += dot_nt(a[i][...], wo[scal[i], :, :width])
    h1[...] = total
    normal, _ = normal_rows(total)
    xn2[...] = (normal * vec[2:3, :] + vec[3:4, :]).astype(BF)
    h2[...] = total + vec[5:6, :]
    units = w1.shape[2]
    for z in range(4):
        wait_all(loads[1 + z])

        def step(j, carry):
            at = pl.ds(pl.multiple_of(j * SUB, SUB), SUB)
            u = dot_nn(xn2[...], w1[z, :, at]) + ub[z, :, at]
            g = (u * gelu_share(u)).astype(BF)
            h2[...] += dot_nt(g, w2[z, :, at])
            return carry

        lax.fori_loop(0, units // SUB, step, 0)
    if not last:
        normal, _ = normal_rows(h2[...])
        outs[2][...] = (normal * vec[8:9, :] + vec[9:10, :]).astype(BF)


def post_fwd(scal, a, hidden, vec, ub, parts, specs, last):
    rows, d = hidden.shape
    units = ub.shape[2]
    anyspec = pl.BlockSpec(memory_space=pl.ANY)
    v = pl.BlockSpec(memory_space=pltpu.VMEM)
    out = [jax.ShapeDtypeStruct((rows, d), F32)] * 2 + ([] if last else [jax.ShapeDtypeStruct((rows, d), BF)])
    return pl.pallas_call(
        functools.partial(post_fwd_kernel, specs, last),
        out_shape=out,
        in_specs=[pl.BlockSpec(memory_space=pltpu.SMEM)] + [v] * 7 + [anyspec] * len(parts),
        out_specs=[v] * len(out),
        scratch_shapes=[
            pltpu.VMEM((4, d, PAD), BF), pltpu.VMEM((4, d, units), BF), pltpu.VMEM((4, d, units), BF),
            pltpu.VMEM((rows, d), BF), pltpu.SemaphoreType.DMA((5,)),
        ],
        compiler_params=pltpu.CompilerParams(vmem_limit_bytes=VMEM_LIMIT),
        cost_estimate=cost(16),
        name="rows_forward",
    )(scal, *a, hidden, vec, ub, *parts)


def post_bwd_kernel(specs, groups, *refs):
    scal = refs[0]
    a, (h1, gy, vec, ub) = refs[1:5], refs[5:9]
    parts, rest = refs[9:9 + len(specs)], refs[9 + len(specs):]
    gy1, dub, dvec = rest[:3]
    da_out = rest[3:7]
    outs = rest[7:7 + len(groups)]
    wo, w1, w2, dwo, dw1, dw2, xn2, df, xn2t, dft, dxn2, sems, osem = rest[7 + len(groups):]
    loads = start_weights(scal, parts, specs, wo, w1, w2, sems)
    rows_d = parts[0].shape[1]
    width = a[0].shape[1]
    places = []
    for out, chunks in zip(outs, groups):
        for i, chunk in enumerate(chunks):
            places.append((out.at[i], pl.ds(pl.multiple_of(scal[4 + chunk] * rows_d, rows_d), rows_d)))
    normal, inverse = normal_rows(h1[...])
    xlow = (normal * vec[2:3, :] + vec[3:4, :]).astype(BF)
    xn2[...] = xlow
    xn2t[...] = xlow.T
    low = gy[...].astype(BF)
    df[...] = low
    dft[...] = low.T
    dvec[...] = jnp.zeros_like(dvec)
    dvec[5:6, :] = jnp.sum(low.astype(F32), axis=0, keepdims=True)
    dxn2[...] = jnp.zeros_like(dxn2)
    units = w1.shape[2]
    stores = []
    for z in range(4):
        wait_all(loads[1 + z])

        def step(j, carry):
            at = pl.ds(pl.multiple_of(j * SUB, SUB), SUB)
            u = dot_nn(xn2[...], w1[z, :, at]) + ub[z, :, at]
            share = gelu_share(u)
            g = (u * share).astype(BF)
            dg = dot_nn(df[...], w2[z, :, at])
            slope = share + u * jnp.exp(-0.5 * u * u) * (1.0 / math.sqrt(2.0 * math.pi))
            du = (dg * slope).astype(BF)
            dub[z, :, at] = jnp.sum(du.astype(F32), axis=0, keepdims=True)
            dw1[z, :, at] = dot_nn(xn2t[...], du).astype(BF)
            dw2[z, :, at] = dot_nn(dft[...], g).astype(BF)
            dxn2[...] += dot_nt(du, w1[z, :, at])
            return carry

        lax.fori_loop(0, units // SUB, step, 0)
        for out, at in places:
            for i, src in enumerate((dw1, dw2)):
                stores.append(pltpu.make_async_copy(src.at[z, at], out.at[z, :, i * units:(i + 1) * units], osem))
                stores[-1].start()
    wait_all(loads[0])
    upstream = dxn2[...]
    dvec[2:3, :] = jnp.sum(upstream * normal, axis=0, keepdims=True)
    dvec[3:4, :] = jnp.sum(upstream, axis=0, keepdims=True)
    total = gy[...] + norm_back(upstream, normal, inverse, vec[2:3, :])
    gy1[...] = total
    low = total.astype(BF)
    dvec[4:5, :] = jnp.sum(low.astype(F32), axis=0, keepdims=True)
    dat = low.T
    dwo[...] = jnp.zeros_like(dwo)
    for i in range(4):
        slot = scal[i]
        dwo[slot, :, :width] = dot_nn(dat, a[i][...]).astype(BF)
        da_out[i][...] = dot_nn(low, wo[slot, :, :width]).astype(BF)
    for out, at in places:
        for z in range(4):
            stores.append(pltpu.make_async_copy(dwo.at[z, at], out.at[z, :, 2 * units:], osem))
            stores[-1].start()
    wait_all(stores)


def post_bwd(scal, a, h1, gy, vec, ub, parts, specs, groups):
    rows, d = h1.shape
    rows_d, width, units = parts[0].shape[1], a[0].shape[1], ub.shape[2]
    anyspec = pl.BlockSpec(memory_space=pl.ANY)
    v = pl.BlockSpec(memory_space=pltpu.VMEM)
    out = [jax.ShapeDtypeStruct((rows, d), F32), jax.ShapeDtypeStruct((4, 1, units), F32), jax.ShapeDtypeStruct((8, d), F32)]
    out += [jax.ShapeDtypeStruct((rows, width), BF)] * 4
    out += [jax.ShapeDtypeStruct((len(chunks), 4, rows_d, 2 * units + PAD), BF) for chunks in groups]
    matrix = pltpu.VMEM((4, d, units), BF)
    thin = pltpu.VMEM((4, d, PAD), BF)
    return pl.pallas_call(
        functools.partial(post_bwd_kernel, specs, groups),
        out_shape=out,
        in_specs=[pl.BlockSpec(memory_space=pltpu.SMEM)] + [v] * 8 + [anyspec] * len(parts),
        out_specs=[v] * 7 + [anyspec] * len(groups),
        scratch_shapes=[
            thin, matrix, matrix, thin, matrix, matrix,
            pltpu.VMEM((rows, d), BF), pltpu.VMEM((rows, d), BF), pltpu.VMEM((d, rows), BF), pltpu.VMEM((d, rows), BF),
            pltpu.VMEM((rows, d), F32), pltpu.SemaphoreType.DMA((5,)), pltpu.SemaphoreType.DMA(()),
        ],
        compiler_params=pltpu.CompilerParams(vmem_limit_bytes=VMEM_LIMIT),
        cost_estimate=cost(33),
        name="rows_backward",
    )(scal, *a, h1, gy, vec, ub, *parts)


MOMENTUM = 0.9
AVERAGE_KEEP = 0.9
WEIGHT_DECAY = 0.0001
RATE_SCALE = 0.02
ROWS_AXES = ("y", "x", "c")
COLS_AXES = ("h", "b")
EVERY = ROWS_AXES + COLS_AXES


def swap(value, name):
    return lax.ppermute(value, name, [(0, 1), (1, 0)])


def home(value):
    return lax.ppermute(value, ("c", "h"), [(0, 0), (1, 2), (2, 1), (3, 3)])


def corner(value):
    return lax.ppermute(value, ("c", "b"), [(0, 3), (1, 2), (2, 1), (3, 0)])


def diagonal(value):
    return lax.ppermute(value, ("y", "x"), [(0, 3), (1, 2), (2, 1), (3, 0)])


def line_corner(value):
    return lax.ppermute(value, ("h", "b"), [(0, 3), (1, 2), (2, 1), (3, 0)])


def double(value, name):
    return jnp.concatenate([value, swap(value, name)], axis=0)


def f32(value):
    return value.astype(F32)


def after(value, *others):
    return lax.optimization_barrier((value,) + others)[0]


def reduce_plane(keep, rest, for_x, for_y):
    def pair(chunk, half):
        return f32(keep[chunk, half]) + f32(rest[chunk, half])

    whole = slice(0, 4)
    to_x = pair(1, whole) + jnp.pad(f32(for_x), ((2, 0), (0, 0), (0, 0)))
    to_y = pair(2, whole) + jnp.pad(f32(for_y), ((0, 2), (0, 0), (0, 0)))
    return (lambda: pair(0, whole)), swap(to_x.astype(BF), "x"), swap(to_y.astype(BF), "y")


def scatter(value):
    value = lax.psum_scatter(f32(value), COLS_AXES, scatter_dimension=0, tiled=True)[0]
    return lax.psum_scatter(value, ROWS_AXES, scatter_dimension=0, tiled=True)


def sgd_step(weight, gradient, moment, average, step_rate):
    decayed = gradient + WEIGHT_DECAY * weight
    moment_next = MOMENTUM * moment + decayed
    weight_next = weight - step_rate * (decayed + MOMENTUM * moment_next)
    average_next = AVERAGE_KEEP * average + (1.0 - AVERAGE_KEEP) * weight_next
    return (weight_next, moment_next, average_next)


def local(
    tokens_in, cotangent, lengths, segments, bucket_map, bucket_tokens,
    attention, feedforward, vectors, head_bias, unit_bias,
    attention_moment, feedforward_moment, vectors_moment, head_moment, unit_moment,
    attention_mean, feedforward_mean, vectors_mean, head_mean, unit_mean,
):
    rows, width_d = tokens_in.shape
    layer_count = attention.shape[0]
    iy, ix, ic, ih, ib = (lax.axis_index(name) for name in EVERY)
    x_size = lax.axis_size("x")
    fast = lax.axis_size("y") == 2 and x_size == 2
    dp_size = lax.axis_size("y") * x_size * 2
    dp_place = (iy * x_size + ix) * 2 + ic
    mp_place = 2 * ih + ib
    quarter = 2 * ic + ib
    stays = ic == ih
    pack_length = rows * 4
    nb = pack_length // BLK

    low_attention, low_feedforward, low_vectors, low_head, low_unit = lax.optimization_barrier(
        tuple(p.astype(BF) for p in (attention, feedforward, vectors, head_bias, unit_bias))
    )
    head_width, units = attention.shape[3], feedforward.shape[3]
    qkv_low = jnp.concatenate([low_attention[:, i] for i in range(3)], axis=2)
    rows_w = attention.shape[2]
    spare_width = units // rows_w if fast else 0
    spare = jnp.zeros((layer_count, rows_w, PAD - head_width - spare_width), BF)
    if fast:
        spare = jnp.concatenate([low_unit.reshape(layer_count, rows_w, spare_width), spare], axis=2)
    ff_low = [
        jnp.concatenate([low_feedforward[layer, 0], low_feedforward[layer, 1],
                         low_attention[layer, 3], spare[layer]], axis=1)
        for layer in range(layer_count)
    ]

    hidden_low = home(tokens_in)
    meta = jnp.concatenate([segments[0], jnp.sum(lengths[0])[None], bucket_map])
    meta = jnp.where(stays, meta, swap(meta, "c"))
    segment_row, total_live, bucket = meta[:pack_length], meta[pack_length], meta[pack_length + 1]

    if fast:
        v8 = double(double(double(low_vectors.reshape(1, layer_count * 6, -1), "c"), "x"), "y")
        v8 = v8.reshape(2, 2, 2, layer_count * 6, -1)
        for axis, place in ((0, iy), (1, ix), (2, ic)):
            v8 = jnp.where(place == 1, jnp.flip(v8, axis), v8)
        full_vectors = v8.reshape(8, layer_count * 6, -1).transpose(1, 0, 2).reshape(layer_count, 6, width_d)
        head_pad = jnp.pad(low_head, ((0, 0), (0, 14), (0, 2 * head_width)))
        packed = jnp.concatenate([qkv_low, head_pad], axis=1)
        far = swap(packed, "h")
        mine, theirs = jnp.where(stays, packed, far), jnp.where(stays, far, packed)
        heads_used = mine[:, rows_w:rows_w + 2, :head_width]
        both_cores = jnp.stack([mine[:, :rows_w], swap(theirs[:, :rows_w], "c")])
        across = swap(both_cores, "x")
        qkv_parts = [both_cores, across, swap(both_cores, "y"), swap(across, "y")]
        chunk_places = [dp_place ^ (2 * (p % 4) + p // 4) for p in range(8)]
        turned = [2 * (i % 2) + i // 2 for i in range(4)]
        slots = jnp.stack([jnp.where(stays, turned[i], turned[i ^ 2]) for i in range(4)])
        specs = [(0, 0, 4), (1, 0, 4), (2, 0, 4), (3, 0, 2), (3, 2, 2)]
        specs = tuple(specs + [(chunk + 4, first, count) for chunk, first, count in specs])
        groups = ((0, 1, 2, 3), (7,), (4, 5, 6))
    else:
        full_vectors = lax.all_gather(low_vectors, ROWS_AXES, axis=2, tiled=True)
        units4 = lax.all_gather(low_unit, COLS_AXES, axis=0)
        heads_used = lax.all_gather(low_head, COLS_AXES, axis=0)[quarter]
        qkv_parts = [lax.all_gather(lax.all_gather(qkv_low, ROWS_AXES, axis=1, tiled=True), COLS_AXES, axis=0)[quarter][None]]
        whole_ff = [lax.all_gather(lax.all_gather(w, ROWS_AXES, axis=0, tiled=True), COLS_AXES, axis=0) for w in ff_low]
        chunk_places = [jnp.int32(0)]
        slots = jnp.stack([quarter ^ i for i in range(4)])
        specs = ((0, 0, 4),)
        groups = ((0,),)
    vec = f32(full_vectors)
    head_rows = f32(heads_used)

    positions = jnp.arange(pack_length, dtype=jnp.int32)
    own_segment = jnp.where(positions < total_live, segment_row, 64 + positions)
    by_block = own_segment.reshape(nb, BLK)
    first_block = jnp.sum(own_segment[None, :] < by_block[:, :1], axis=1) // BLK
    end_block = (jnp.sum(own_segment[None, :] <= by_block[:, -1:], axis=1) + BLK - 1) // BLK
    places = jnp.stack([quarter ^ rel for rel in range(4)])
    chunk_array = jnp.stack(chunk_places).astype(jnp.int32)
    scal = jnp.concatenate([first_block, end_block, places, jnp.zeros((1,), jnp.int32), chunk_array]).astype(jnp.int32)
    scal_rows = jnp.concatenate([slots.astype(jnp.int32), chunk_array])
    segk, segq = own_segment[:, None], own_segment[None, :]
    live_own = (quarter * rows + jnp.arange(rows) < total_live)[:, None]
    counts_float = f32(bucket_tokens)
    chosen = jnp.arange(bucket_tokens.shape[0]) == bucket
    pack_weight = bucket_tokens.shape[0] * jnp.sum(jnp.where(chosen, counts_float, 0.0)) / jnp.sum(counts_float)

    def vec_rows(layer, other):
        return jnp.concatenate([vec[layer], jnp.zeros((2, width_d), F32), vec[other], jnp.zeros((2, width_d), F32)])

    hidden = f32(hidden_low)
    normal, _ = normal_rows(hidden)
    normed = (normal * vec[0, 0] + vec[0, 1]).astype(BF)
    saved = []
    if fast:
        line = double(double(ff_low[0][None], "h"), "b")
        x_part, y_part = swap(line, "x"), swap(line, "y")
    for layer in range(layer_count):
        last = layer == layer_count - 1
        over = swap(normed, "b")
        normed_parts = [normed, over, swap(normed, "c"), swap(over, "c")]
        if fast:
            if layer:
                normed_parts, x_part, y_part = lax.optimization_barrier((normed_parts, x_part, y_part))
            if not last:
                ahead = after(ff_low[layer + 1][None], *normed_parts)
                ahead_h = swap(ahead, "h")
            own_parts = [line, x_part, y_part]
            if layer:
                own_parts += [swap(y_part[:2], "x"), swap(x_part[2:], "y")]
        mixed, log_total = attn_fwd(scal, normed_parts, qkv_parts, layer, head_rows[layer], segk, segq)
        if fast:
            if not last:
                mixed, ahead_h = lax.optimization_barrier((mixed, ahead_h))
            if layer:
                mixed, own_parts = lax.optimization_barrier((mixed, own_parts))
            else:
                mixed, x_part, y_part = lax.optimization_barrier((mixed, x_part, y_part))
                own_parts = [line, x_part, y_part, swap(y_part[:2], "x"), swap(x_part[2:], "y")]
        own_mixed = [mixed[0], swap(mixed[1], "b"), swap(mixed[2], "c"), corner(mixed[3])]
        vec16 = vec_rows(layer, 0 if last else layer + 1)
        if fast:
            at = 2 * units + head_width
            unit_row = f32(line[:, :, at:at + spare_width].reshape(4, 1, units))
            parts = own_parts + [swap(part, "c") for part in own_parts]
            if not last:
                ahead = jnp.concatenate([ahead, ahead_h])
                ahead_b = swap(after(ahead, *own_mixed), "b")
                own_mixed, ahead_b = lax.optimization_barrier((own_mixed, ahead_b))
                line = jnp.concatenate([ahead, ahead_b])
                x_part, y_part = swap(line, "x"), swap(line, "y")
        else:
            parts = [whole_ff[layer]]
            unit_row = f32(units4[:, layer][:, None, :])
        outs = post_fwd(scal_rows, own_mixed, hidden, vec16, unit_row, parts, specs, last)
        saved.append((hidden, normed_parts, mixed, log_total, own_mixed, outs[0], unit_row, vec16, parts))
        hidden = outs[1]
        if not last:
            normed = outs[2]
    hidden_out = f32(home(jnp.where(live_own, hidden, 0.0).astype(BF)))
    hidden_out = jnp.where(stays, jnp.where(live_own, hidden, 0.0), hidden_out)

    cotangent_here = home(after(cotangent, saved[0][5]))
    upstream = jnp.where(live_own, f32(cotangent_here) * pack_weight, 0.0)
    qkv_grads, matrix_grads, vector_grads, head_grads, unit_grads = [], [], [], [], []
    waiting = None
    for layer in reversed(range(layer_count)):
        hidden, normed_parts, mixed, log_total, own_mixed, middle, unit_row, vec16, parts = saved[layer]
        outs = post_bwd(scal_rows, own_mixed, middle, upstream, vec16, unit_row, parts, specs, groups)
        if waiting is not None:
            outs, beside = lax.optimization_barrier((outs, waiting[1:]))
            own = waiting[0]() + f32(beside[0]) + f32(beside[1])
        upstream, d_unit, d_vec = outs[:3]
        d_mixed, terms = outs[3:7], outs[7:]
        d_parts = [d_mixed[0], swap(d_mixed[1], "b"), swap(d_mixed[2], "c"), corner(d_mixed[3])]
        if fast:
            keep, send_far, send = terms
            far_sum = (f32(keep[3]) + f32(swap(send_far, "c")[0])).astype(BF)
            rest = swap(after(send, *d_parts), "c")
            for_x, for_y = swap(far_sum[2:], "y"), swap(far_sum[:2], "x")
            if waiting is not None:
                to_b = swap(after(own[2:].astype(BF), *d_parts), "b")
        outs = attn_bwd(scal, normed_parts, qkv_parts, layer, d_parts, mixed, head_rows[layer], segk, segq, log_total)
        if fast:
            outs, rest, for_x, for_y = lax.optimization_barrier((outs, rest, for_x, for_y))
            if waiting is not None:
                outs, to_b = lax.optimization_barrier((outs, to_b))
                above = own[:2] + f32(to_b)
            waiting = reduce_plane(keep, rest, for_x, for_y)
        else:
            matrix_grads.append(scatter(terms[0][0]))
        d_rows, d_head = outs[:2]
        qkv_grads.append(outs[2:])
        got = swap(d_rows[2:4], "c")
        got2 = swap((f32(d_rows[1]) + f32(got[1])).astype(BF), "b")
        d_normed = f32(d_rows[0]) + f32(got[0]) + f32(got2)
        normal, inverse = normal_rows(hidden)
        upstream = upstream + norm_back(d_normed, normal, inverse, vec[layer, 0])
        vector_grads.append(jnp.concatenate([
            jnp.sum(d_normed * normal, axis=0)[None], jnp.sum(d_normed, axis=0)[None], d_vec[2:6]]))
        head_grads.append(d_head)
        unit_grads.append(d_unit[:, 0])
    vector_sum = jnp.stack(vector_grads[::-1])
    head_sum = jnp.stack(head_grads[::-1])
    unit_sum = jnp.stack(unit_grads[::-1], axis=1)
    v_size, u_size = vector_sum.size, unit_sum.size // 4
    if fast:
        by_core = [jnp.stack([grads[core] for grads in qkv_grads[::-1]]) for core in range(2)]
        other = swap(by_core[1], "c")
        above_h = swap(after(above[1].astype(BF), got2), "h")
        beside, other = lax.optimization_barrier((waiting[1:], other))
        own = waiting[0]() + f32(beside[0]) + f32(beside[1])
        to_hb, to_b = swap(own[3].astype(BF), "b"), swap(own[2].astype(BF), "b")
        to_hb, above_h, returned = lax.optimization_barrier((to_hb, above_h, home(upstream.astype(BF))))
        hop_h = (own[1] + f32(to_hb)).astype(BF)
        hop_h, vector_sum, other = lax.optimization_barrier((hop_h, vector_sum, other))
        to_h = swap(hop_h, "h")
        both = jnp.stack([jnp.where(stays, by_core[0], other), jnp.where(stays, other, by_core[0])])
        sides = swap(both[:, :, 1], "x"), swap(both[:, :, 2], "y"), diagonal(both[:, :, 3])
        flat_v, flat_e, flat_u = vector_sum.reshape(-1), head_sum.reshape(-1), unit_sum.reshape(4, -1)
        near_e = jnp.where(stays, flat_e, 0.0)
        got_h = swap(jnp.concatenate([flat_v, flat_u[1], flat_e - near_e]), "h")
        got_b = swap(jnp.concatenate([flat_v, flat_u[2]]), "b")
        got_hb = line_corner(jnp.concatenate([flat_v, flat_u[3]]))
        flat = jnp.concatenate([flat_v, flat_u[0], near_e]) + got_h + jnp.pad(got_b + got_hb, (0, flat_e.size))
        others = swap(flat, "x"), swap(flat, "y"), diagonal(flat)
        sides, to_b, to_h = lax.optimization_barrier((sides, to_b, to_h))
        both = f32(both[:, :, 0]) + f32(sides[0]) + f32(sides[1]) + f32(sides[2])
        qkv_gradient = both[0] + f32(swap(both[1].astype(BF), "h"))
        flat = flat + others[0] + others[1] + others[2]
        flat = flat + swap(flat, "c")
        vector_total = flat[:v_size].reshape(vector_sum.shape)
        unit_gradient = flat[v_size:v_size + u_size].reshape(unit_bias.shape)
        head_gradient = flat[v_size + u_size:].reshape(head_bias.shape)
        matrix_grads += [above[0] + f32(above_h), own[0] + f32(to_b) + f32(to_h)]
    else:
        empty = jnp.zeros((4,) + qkv_grads[0][0].shape[1:], F32)
        qkv_gradient = jnp.stack([scatter(empty.at[quarter].set(f32(grads[0][0]))) for grads in qkv_grads[::-1]])
    matrix_gradient = jnp.stack(matrix_grads[::-1])
    attention_gradient = jnp.stack(
        [qkv_gradient[:, :, i * head_width:(i + 1) * head_width] for i in range(3)]
        + [matrix_gradient[:, :, 2 * units:2 * units + head_width]], axis=1)
    feedforward_gradient = jnp.stack([matrix_gradient[:, :, :units], matrix_gradient[:, :, units:2 * units]], axis=1)

    if not fast:
        placed = jnp.zeros((4,) + head_sum.shape, F32).at[quarter].set(head_sum)
        vector_total, unit_total, head_total = lax.psum((vector_sum, unit_sum, placed), EVERY)
        unit_gradient, head_gradient = unit_total[mp_place], head_total[mp_place]
    chunk = width_d // dp_size
    vectors_gradient = lax.dynamic_slice_in_dim(vector_total, dp_place * chunk, chunk, 2)

    if not fast:
        returned = home(upstream.astype(BF))
    input_gradient = jnp.where(stays, upstream, f32(returned))
    step_rate = RATE_SCALE * lax.rsqrt(jnp.float32(dp_size * pack_length))
    weights = (attention, feedforward, vectors, head_bias, unit_bias)
    gradients = (attention_gradient, feedforward_gradient, vectors_gradient, head_gradient, unit_gradient)
    moments = (attention_moment, feedforward_moment, vectors_moment, head_moment, unit_moment)
    averages = (attention_mean, feedforward_mean, vectors_mean, head_mean, unit_mean)
    steps = [sgd_step(*leaf, step_rate) for leaf in zip(weights, gradients, moments, averages)]
    return (
        (hidden_out, input_gradient) + gradients + tuple(s[0] for s in steps) + tuple(s[1] for s in steps)
        + tuple(s[2] for s in steps) + (steps[0][0].astype(BF), steps[1][0].astype(BF))
    )


def solution(mesh):
    dp_size = mesh.shape["dp"]
    inner = jax.sharding.Mesh(mesh.devices.reshape(2, dp_size // 4, 2, 2, 2), EVERY)
    rows, cols = ROWS_AXES, COLS_AXES
    tokens = P(rows + cols, None)
    params = (P(None, None, rows, cols), P(None, None, rows, cols), P(None, None, rows), P(None, None, cols), P(None, cols))
    in_specs = (tokens, tokens, P(rows, None), P(rows, None), P(rows), P()) + params * 3
    out_specs = (tokens, tokens) + params * 4 + params[:2]
    return jax.shard_map(local, mesh=inner, in_specs=in_specs, out_specs=out_specs, check_vma=False)
```

```python
import functools, math
import jax, jax.numpy as jnp
from jax import lax
from jax.experimental import pallas as pl
from jax.experimental.pallas import tpu as pltpu
from jax.sharding import PartitionSpec as P

HEAD_DIM = 32
MASKED = -1e30
LOG2E = math.log2(math.e)
SCORE = HEAD_DIM ** (-0.5)
SCORE2 = SCORE * LOG2E
BLK = 256
BF = jnp.bfloat16
F32 = jnp.float32
VMEM_LIMIT = 60 * 1024 * 1024


def cost(micros):
    return pl.CostEstimate(flops=micros * 1100000000, bytes_accessed=1000000, transcendentals=0)


def dot_nn(a, b):
    return lax.dot_general(a, b, (((1,), (0,)), ((), ())), preferred_element_type=F32)


def dot_nt(a, b):
    return lax.dot_general(a, b, (((1,), (1,)), ((), ())), preferred_element_type=F32)


def load_parts(scal, parts, dest, first, rows, sem):
    copies = []
    for i, part in enumerate(parts):
        start = pl.multiple_of(scal[first + i] * rows, rows)
        copies.append(pltpu.make_async_copy(part, dest.at[pl.ds(start, rows)], sem))
    for copy in copies:
        copy.start()
    return copies


def chunks_of(wrefs, layer):
    return [w.at[core, layer] for core in range(wrefs[0].shape[0]) for w in wrefs]


def attn_fwd_kernel(nb, nw, layer, *refs):
    scal = refs[0]
    xparts = refs[1:5]
    wparts = chunks_of(refs[5:5 + nw], layer)
    bias, segk, segq, out, lse = refs[5 + nw:10 + nw]
    xs, ws, ks, qt, vt, acc, scores, sems = refs[10 + nw:]
    heads = ks.shape[0]
    width = heads * HEAD_DIM
    rows = xparts[0].shape[0]
    base = 2 * nb
    wcopies = load_parts(scal, wparts, ws, base + 5, wparts[0].shape[0], sems.at[4])
    xcopies = [load_parts(scal, [p], xs, base + i, rows, sems.at[i])[0] for i, p in enumerate(xparts)]
    for c in wcopies:
        c.wait()
    for i in range(4):
        xcopies[i].wait()
        start = pl.multiple_of(scal[base + i] * rows, rows)
        y = dot_nn(xs[pl.ds(start, rows), :], ws[...])
        qt[:, pl.ds(start, rows)] = (y[:, :width] + bias[0:1, :]).T.astype(BF)
        k = y[:, width:2 * width].astype(BF)
        for h in range(heads):
            ks[h, pl.ds(start, rows), :] = k[:, h * HEAD_DIM:(h + 1) * HEAD_DIM]
        vt[:, pl.ds(start, rows)] = (y[:, 2 * width:] + bias[1:2, :]).T.astype(BF)
    lse[...] = jnp.zeros_like(lse)
    per = rows // BLK

    def fold(z):
        return z.reshape(BLK // 8, 8, BLK)

    def q_block(qb, carry):
        q0 = pl.multiple_of(qb * BLK, BLK)
        acc[...] = jnp.zeros_like(acc)
        sq = segq[:, pl.ds(q0, BLK)]
        first, end = scal[qb], scal[nb + qb]

        def score_block(kb, ms):
            k0 = pl.multiple_of(kb * BLK, BLK)
            mask = segk[pl.ds(k0, BLK), :] == sq
            new = []
            for h in range(heads):
                hs = slice(h * HEAD_DIM, (h + 1) * HEAD_DIM)
                s = dot_nn(ks[h, pl.ds(k0, BLK), :], qt[hs, pl.ds(q0, BLK)])
                s = jnp.where(mask, s, MASKED)
                scores[h, kb] = s
                new.append(jnp.maximum(ms[h], jnp.max(fold(s), axis=0)))
            return tuple(new)

        ms = lax.fori_loop(first, end, score_block, (jnp.full((8, BLK), MASKED, F32),) * heads)
        tops = [jnp.max(m, axis=0, keepdims=True) * SCORE2 for m in ms]

        def mix_block(kb, ls):
            k0 = pl.multiple_of(kb * BLK, BLK)
            new = []
            for h in range(heads):
                hs = slice(h * HEAD_DIM, (h + 1) * HEAD_DIM)
                p = jnp.exp2(scores[h, kb] * SCORE2 - tops[h])
                acc[hs, :] += dot_nn(vt[hs, pl.ds(k0, BLK)], p.astype(BF))
                new.append(ls[h] + jnp.sum(fold(p), axis=0))
            return tuple(new)

        ls = lax.fori_loop(first, end, mix_block, (jnp.zeros((8, BLK), F32),) * heads)
        for h in range(heads):
            hs = slice(h * HEAD_DIM, (h + 1) * HEAD_DIM)
            l = jnp.sum(ls[h], axis=0, keepdims=True)
            acc[hs, :] = acc[hs, :] * (1.0 / l)
            lse[h:h + 1, pl.ds(q0, BLK)] = tops[h] + jnp.log2(l)
        part = lax.bitwise_xor(lax.div(qb, per), scal[base])
        out[part, pl.ds(pl.multiple_of(lax.rem(qb, per) * BLK, BLK), BLK), :] = acc[...].T.astype(BF)
        return carry

    lax.fori_loop(0, nb, q_block, 0)


def attn_fwd(scal, xparts, wparts, layer, bias, segk, segq):
    rows, d = xparts[0].shape
    t = 4 * rows
    width = wparts[0].shape[3] // 3
    heads = width // HEAD_DIM
    nb = t // BLK
    npc = len(wparts)
    anyspec = pl.BlockSpec(memory_space=pl.ANY)
    v = pl.BlockSpec(memory_space=pltpu.VMEM)
    return pl.pallas_call(
        functools.partial(attn_fwd_kernel, nb, npc, layer),
        out_shape=(jax.ShapeDtypeStruct((4, rows, width), BF), jax.ShapeDtypeStruct((8, t), F32)),
        in_specs=[pl.BlockSpec(memory_space=pltpu.SMEM)] + [anyspec] * (4 + npc) + [v] * 3,
        out_specs=(v, v),
        scratch_shapes=[
            pltpu.VMEM((t, d), BF), pltpu.VMEM((d, 3 * width), BF), pltpu.VMEM((heads, t, HEAD_DIM), BF),
            pltpu.VMEM((width, t), BF), pltpu.VMEM((width, t), BF), pltpu.VMEM((width, BLK), F32),
            pltpu.VMEM((heads, nb, BLK, BLK), F32),
            pltpu.SemaphoreType.DMA((5,)),
        ],
        compiler_params=pltpu.CompilerParams(vmem_limit_bytes=VMEM_LIMIT),
        cost_estimate=cost(28),
        name="attention_forward",
    )(scal, *xparts, *wparts, bias, segk, segq)


def attn_bwd_kernel(nb, nw, layer, *refs):
    scal = refs[0]
    xparts = refs[1:5]
    groups = refs[5].shape[0]
    wparts = chunks_of(refs[5:5 + nw], layer)
    npc = len(wparts)
    daparts = refs[5 + nw:9 + nw]
    a_saved, bias, segk, segq, lse, dx, dbias = refs[9 + nw:16 + nw]
    dw_out = refs[16 + nw:16 + nw + groups]
    xs, ws, qs, ks, vs, das, qt, kt, dat, delta, dqt, dall, dka, dva, dw, sems, osem = refs[16 + nw + groups:]
    heads = ks.shape[0]
    width = heads * HEAD_DIM
    rows = xparts[0].shape[0]
    base = 2 * nb
    wcopies = load_parts(scal, wparts, ws, base + 5, wparts[0].shape[0], sems.at[4])
    xcopies = [load_parts(scal, [p], xs, base + i, rows, sems.at[i])[0] for i, p in enumerate(xparts)]
    for c in wcopies:
        c.wait()
    for i in range(4):
        xcopies[i].wait()
        start = pl.multiple_of(scal[base + i] * rows, rows)
        at = pl.ds(start, rows)
        x = xs[at, :]
        y = dot_nn(x, ws[...])
        q = y[:, :width] + bias[0:1, :]
        qt[:, at] = q.T.astype(BF)
        ql = q.astype(BF)
        kf = y[:, width:2 * width]
        kt[:, at] = kf.T.astype(BF)
        kl = kf.astype(BF)
        vl = (y[:, 2 * width:] + bias[1:2, :]).astype(BF)
        dal = daparts[i][...]
        daf = dal.astype(F32).T
        dat[:, at] = daf.astype(BF)
        prod = daf * a_saved[i].astype(F32).T
        for h in range(heads):
            hs = slice(h * HEAD_DIM, (h + 1) * HEAD_DIM)
            qs[h, at, :] = ql[:, hs]
            ks[h, at, :] = kl[:, hs]
            vs[h, at, :] = vl[:, hs]
            das[h, at, :] = dal[:, hs]
            delta[h:h + 1, at] = jnp.sum(prod[hs, :], axis=0, keepdims=True)
    dqt[...] = jnp.zeros_like(dqt)

    def k_block(kb, carry):
        k0 = pl.multiple_of(kb * BLK, BLK)
        kat = pl.ds(k0, BLK)
        dka[...] = jnp.zeros_like(dka)
        dva[...] = jnp.zeros_like(dva)
        sk = segk[kat, :]

        def q_block(qb, c2):
            q0 = pl.multiple_of(qb * BLK, BLK)
            qat = pl.ds(q0, BLK)
            mask = sk == segq[:, qat]
            for h in range(heads):
                hs = slice(h * HEAD_DIM, (h + 1) * HEAD_DIM)
                s = dot_nn(ks[h, kat, :], qt[hs, qat])
                p = jnp.where(mask, jnp.exp2(s * SCORE2 - lse[h:h + 1, qat]), 0.0)
                dp = dot_nn(vs[h, kat, :], dat[hs, qat])
                dva[h] += dot_nn(p.astype(BF), das[h, qat, :])
                ds = (p * (dp - delta[h:h + 1, qat])).astype(BF)
                dka[h] += dot_nn(ds, qs[h, qat, :])
                dqt[hs, qat] += dot_nn(kt[hs, kat], ds)
            return c2

        lax.fori_loop(scal[kb], scal[nb + kb], q_block, 0)
        for h in range(heads):
            hs = slice(h * HEAD_DIM, (h + 1) * HEAD_DIM)
            dall[width + h * HEAD_DIM:width + (h + 1) * HEAD_DIM, kat] = (dka[h].T * SCORE).astype(BF)
            dall[2 * width + h * HEAD_DIM:2 * width + (h + 1) * HEAD_DIM, kat] = dva[h].T.astype(BF)
        return carry

    lax.fori_loop(0, nb, k_block, 0)
    dall[:width, :] = (dqt[...] * SCORE).astype(BF)
    dbias[0:1, :] = jnp.sum(dall[:width, :].astype(F32), axis=1)[None, :]
    dbias[1:2, :] = jnp.sum(dall[2 * width:, :].astype(F32), axis=1)[None, :]
    dw[...] = dot_nn(dall[...], xs[...]).T.astype(dw.dtype)
    rows_d, per = wparts[0].shape[0], npc // groups
    stores = []
    for p in range(npc):
        at = pl.ds(pl.multiple_of(scal[base + 5 + p] * rows_d, rows_d), rows_d)
        stores.append(pltpu.make_async_copy(dw.at[at], dw_out[p // per].at[p % per], osem))
        stores[-1].start()
    for i in range(4):
        start = pl.multiple_of(scal[base + i] * rows, rows)
        at = pl.ds(start, rows)
        dx[i] = dot_nt(dall[:, at].astype(F32).T.astype(BF), ws[...]).astype(BF)
    for copy in stores:
        copy.wait()


def attn_bwd(scal, xparts, wparts, layer, daparts, a_saved, bias, segk, segq, lse):
    rows, d = xparts[0].shape
    t = 4 * rows
    groups, _, rows_w, width = wparts[0].shape
    width //= 3
    heads = width // HEAD_DIM
    nb = t // BLK
    npc = len(wparts)
    anyspec = pl.BlockSpec(memory_space=pl.ANY)
    v = pl.BlockSpec(memory_space=pltpu.VMEM)
    head_rows = pltpu.VMEM((heads, t, HEAD_DIM), BF)
    flat = pltpu.VMEM((width, t), BF)
    return pl.pallas_call(
        functools.partial(attn_bwd_kernel, nb, npc, layer),
        out_shape=(
            jax.ShapeDtypeStruct((4, rows, d), BF),
            jax.ShapeDtypeStruct((2, width), F32),
        ) + (jax.ShapeDtypeStruct((npc, rows_w, 3 * width), BF),) * groups,
        in_specs=[pl.BlockSpec(memory_space=pltpu.SMEM)] + [anyspec] * (4 + npc) + [v] * 9,
        out_specs=(v, v) + (anyspec,) * groups,
        scratch_shapes=[
            pltpu.VMEM((t, d), BF), pltpu.VMEM((d, 3 * width), BF),
            head_rows, head_rows, head_rows, head_rows, flat, flat, flat,
            pltpu.VMEM((8, t), F32), pltpu.VMEM((width, t), F32), pltpu.VMEM((3 * width, t), BF),
            pltpu.VMEM((heads, BLK, HEAD_DIM), F32), pltpu.VMEM((heads, BLK, HEAD_DIM), F32),
            pltpu.VMEM((d, 3 * width), BF), pltpu.SemaphoreType.DMA((5,)), pltpu.SemaphoreType.DMA(()),
        ],
        compiler_params=pltpu.CompilerParams(vmem_limit_bytes=VMEM_LIMIT),
        cost_estimate=cost(55),
        name="attention_backward",
    )(scal, *xparts, *wparts, *daparts, a_saved, bias, segk, segq, lse)


EPSILON = 1e-05
SUB = 640


def normal_rows(hidden):
    centre = hidden - jnp.mean(hidden, axis=-1, keepdims=True)
    inverse = lax.rsqrt(jnp.mean(centre * centre, axis=-1, keepdims=True) + EPSILON)
    return centre * inverse, inverse


def norm_back(upstream, normal, inverse, gain_row):
    scaled = upstream * gain_row
    return inverse * (scaled - jnp.mean(scaled, axis=-1, keepdims=True) - normal * jnp.mean(scaled * normal, axis=-1, keepdims=True))


def gelu_share(u):
    return 0.5 * (1.0 + lax.erf(u * (1.0 / math.sqrt(2.0))))


PAD = 256


def start_weights(scal, parts, specs, wo, w1, w2, sems):
    rows, units = parts[0].shape[1], w1.shape[2]
    by_block = [[] for _ in range(5)]
    for part, (chunk, first, count) in zip(parts, specs):
        at = pl.ds(pl.multiple_of(scal[4 + chunk] * rows, rows), rows)
        for z in range(first, first + count):
            src = part.at[z - first]
            by_block[0].append(pltpu.make_async_copy(src.at[:, 2 * units:], wo.at[z, at], sems.at[0]))
            by_block[1 + z].append(pltpu.make_async_copy(src.at[:, :units], w1.at[z, at], sems.at[1 + z]))
            by_block[1 + z].append(pltpu.make_async_copy(src.at[:, units:2 * units], w2.at[z, at], sems.at[1 + z]))
    for copies in by_block:
        for copy in copies:
            copy.start()
    return by_block


def wait_all(copies):
    for copy in copies:
        copy.wait()


def post_fwd_kernel(specs, last, *refs):
    scal = refs[0]
    a, (hidden, vec, ub) = refs[1:5], refs[5:8]
    parts, rest = refs[8:8 + len(specs)], refs[8 + len(specs):]
    outs, (wo, w1, w2, xn2, sems) = rest[:-5], rest[-5:]
    h1, h2 = outs[:2]
    loads = start_weights(scal, parts, specs, wo, w1, w2, sems)
    wait_all(loads[0])
    width = a[0].shape[1]
    total = hidden[...] + vec[4:5, :]
    for i in range(4):
        total += dot_nt(a[i][...], wo[scal[i], :, :width])
    h1[...] = total
    normal, _ = normal_rows(total)
    xn2[...] = (normal * vec[2:3, :] + vec[3:4, :]).astype(BF)
    h2[...] = total + vec[5:6, :]
    units = w1.shape[2]
    for z in range(4):
        wait_all(loads[1 + z])

        def step(j, carry):
            at = pl.ds(pl.multiple_of(j * SUB, SUB), SUB)
            u = dot_nn(xn2[...], w1[z, :, at]) + ub[z, :, at]
            g = (u * gelu_share(u)).astype(BF)
            h2[...] += dot_nt(g, w2[z, :, at])
            return carry

        lax.fori_loop(0, units // SUB, step, 0)
    if not last:
        normal, _ = normal_rows(h2[...])
        outs[2][...] = (normal * vec[8:9, :] + vec[9:10, :]).astype(BF)


def post_fwd(scal, a, hidden, vec, ub, parts, specs, last):
    rows, d = hidden.shape
    units = ub.shape[2]
    anyspec = pl.BlockSpec(memory_space=pl.ANY)
    v = pl.BlockSpec(memory_space=pltpu.VMEM)
    out = [jax.ShapeDtypeStruct((rows, d), F32)] * 2 + ([] if last else [jax.ShapeDtypeStruct((rows, d), BF)])
    return pl.pallas_call(
        functools.partial(post_fwd_kernel, specs, last),
        out_shape=out,
        in_specs=[pl.BlockSpec(memory_space=pltpu.SMEM)] + [v] * 7 + [anyspec] * len(parts),
        out_specs=[v] * len(out),
        scratch_shapes=[
            pltpu.VMEM((4, d, PAD), BF), pltpu.VMEM((4, d, units), BF), pltpu.VMEM((4, d, units), BF),
            pltpu.VMEM((rows, d), BF), pltpu.SemaphoreType.DMA((5,)),
        ],
        compiler_params=pltpu.CompilerParams(vmem_limit_bytes=VMEM_LIMIT),
        cost_estimate=cost(16),
        name="rows_forward",
    )(scal, *a, hidden, vec, ub, *parts)


def post_bwd_kernel(specs, groups, *refs):
    scal = refs[0]
    a, (h1, gy, vec, ub) = refs[1:5], refs[5:9]
    parts, rest = refs[9:9 + len(specs)], refs[9 + len(specs):]
    gy1, dub, dvec = rest[:3]
    da_out = rest[3:7]
    outs = rest[7:7 + len(groups)]
    wo, w1, w2, dwo, dw1, dw2, xn2, df, xn2t, dft, dxn2, sems, osem = rest[7 + len(groups):]
    loads = start_weights(scal, parts, specs, wo, w1, w2, sems)
    rows_d = parts[0].shape[1]
    width = a[0].shape[1]
    places = []
    for out, chunks in zip(outs, groups):
        for i, chunk in enumerate(chunks):
            places.append((out.at[i], pl.ds(pl.multiple_of(scal[4 + chunk] * rows_d, rows_d), rows_d)))
    normal, inverse = normal_rows(h1[...])
    xlow = (normal * vec[2:3, :] + vec[3:4, :]).astype(BF)
    xn2[...] = xlow
    xn2t[...] = xlow.T
    low = gy[...].astype(BF)
    df[...] = low
    dft[...] = low.T
    dvec[...] = jnp.zeros_like(dvec)
    dvec[5:6, :] = jnp.sum(low.astype(F32), axis=0, keepdims=True)
    dxn2[...] = jnp.zeros_like(dxn2)
    units = w1.shape[2]
    stores = []
    for z in range(4):
        wait_all(loads[1 + z])

        def step(j, carry):
            at = pl.ds(pl.multiple_of(j * SUB, SUB), SUB)
            u = dot_nn(xn2[...], w1[z, :, at]) + ub[z, :, at]
            share = gelu_share(u)
            g = (u * share).astype(BF)
            dg = dot_nn(df[...], w2[z, :, at])
            slope = share + u * jnp.exp(-0.5 * u * u) * (1.0 / math.sqrt(2.0 * math.pi))
            du = (dg * slope).astype(BF)
            dub[z, :, at] = jnp.sum(du.astype(F32), axis=0, keepdims=True)
            dw1[z, :, at] = dot_nn(xn2t[...], du).astype(BF)
            dw2[z, :, at] = dot_nn(dft[...], g).astype(BF)
            dxn2[...] += dot_nt(du, w1[z, :, at])
            return carry

        lax.fori_loop(0, units // SUB, step, 0)
        for out, at in places:
            for i, src in enumerate((dw1, dw2)):
                stores.append(pltpu.make_async_copy(src.at[z, at], out.at[z, :, i * units:(i + 1) * units], osem))
                stores[-1].start()
    wait_all(loads[0])
    upstream = dxn2[...]
    dvec[2:3, :] = jnp.sum(upstream * normal, axis=0, keepdims=True)
    dvec[3:4, :] = jnp.sum(upstream, axis=0, keepdims=True)
    total = gy[...] + norm_back(upstream, normal, inverse, vec[2:3, :])
    gy1[...] = total
    low = total.astype(BF)
    dvec[4:5, :] = jnp.sum(low.astype(F32), axis=0, keepdims=True)
    dat = low.T
    dwo[...] = jnp.zeros_like(dwo)
    for i in range(4):
        slot = scal[i]
        dwo[slot, :, :width] = dot_nn(dat, a[i][...]).astype(BF)
        da_out[i][...] = dot_nn(low, wo[slot, :, :width]).astype(BF)
    for out, at in places:
        for z in range(4):
            stores.append(pltpu.make_async_copy(dwo.at[z, at], out.at[z, :, 2 * units:], osem))
            stores[-1].start()
    wait_all(stores)


def post_bwd(scal, a, h1, gy, vec, ub, parts, specs, groups):
    rows, d = h1.shape
    rows_d, width, units = parts[0].shape[1], a[0].shape[1], ub.shape[2]
    anyspec = pl.BlockSpec(memory_space=pl.ANY)
    v = pl.BlockSpec(memory_space=pltpu.VMEM)
    out = [jax.ShapeDtypeStruct((rows, d), F32), jax.ShapeDtypeStruct((4, 1, units), F32), jax.ShapeDtypeStruct((8, d), F32)]
    out += [jax.ShapeDtypeStruct((rows, width), BF)] * 4
    out += [jax.ShapeDtypeStruct((len(chunks), 4, rows_d, 2 * units + PAD), BF) for chunks in groups]
    matrix = pltpu.VMEM((4, d, units), BF)
    thin = pltpu.VMEM((4, d, PAD), BF)
    return pl.pallas_call(
        functools.partial(post_bwd_kernel, specs, groups),
        out_shape=out,
        in_specs=[pl.BlockSpec(memory_space=pltpu.SMEM)] + [v] * 8 + [anyspec] * len(parts),
        out_specs=[v] * 7 + [anyspec] * len(groups),
        scratch_shapes=[
            thin, matrix, matrix, thin, matrix, matrix,
            pltpu.VMEM((rows, d), BF), pltpu.VMEM((rows, d), BF), pltpu.VMEM((d, rows), BF), pltpu.VMEM((d, rows), BF),
            pltpu.VMEM((rows, d), F32), pltpu.SemaphoreType.DMA((5,)), pltpu.SemaphoreType.DMA(()),
        ],
        compiler_params=pltpu.CompilerParams(vmem_limit_bytes=VMEM_LIMIT),
        cost_estimate=cost(33),
        name="rows_backward",
    )(scal, *a, h1, gy, vec, ub, *parts)


MOMENTUM = 0.9
AVERAGE_KEEP = 0.9
WEIGHT_DECAY = 0.0001
RATE_SCALE = 0.02
ROWS_AXES = ("y", "x", "c")
COLS_AXES = ("h", "b")
EVERY = ROWS_AXES + COLS_AXES


def swap(value, name):
    return lax.ppermute(value, name, [(0, 1), (1, 0)])


def home(value):
    return lax.ppermute(value, ("c", "h"), [(0, 0), (1, 2), (2, 1), (3, 3)])


def corner(value):
    return lax.ppermute(value, ("c", "b"), [(0, 3), (1, 2), (2, 1), (3, 0)])


def diagonal(value):
    return lax.ppermute(value, ("y", "x"), [(0, 3), (1, 2), (2, 1), (3, 0)])


def line_corner(value):
    return lax.ppermute(value, ("h", "b"), [(0, 3), (1, 2), (2, 1), (3, 0)])


def double(value, name):
    return jnp.concatenate([value, swap(value, name)], axis=0)


def f32(value):
    return value.astype(F32)


def after(value, *others):
    return lax.optimization_barrier((value,) + others)[0]


def reduce_plane(keep, rest, for_x, for_y):
    def pair(chunk, half):
        return f32(keep[chunk, half]) + f32(rest[chunk, half])

    whole = slice(0, 4)
    to_x = pair(1, whole) + jnp.pad(f32(for_x), ((2, 0), (0, 0), (0, 0)))
    to_y = pair(2, whole) + jnp.pad(f32(for_y), ((0, 2), (0, 0), (0, 0)))
    return (lambda: pair(0, whole)), swap(to_x.astype(BF), "x"), swap(to_y.astype(BF), "y")


def scatter(value):
    value = lax.psum_scatter(f32(value), COLS_AXES, scatter_dimension=0, tiled=True)[0]
    return lax.psum_scatter(value, ROWS_AXES, scatter_dimension=0, tiled=True)


def sgd_step(weight, gradient, moment, average, step_rate):
    decayed = gradient + WEIGHT_DECAY * weight
    moment_next = MOMENTUM * moment + decayed
    weight_next = weight - step_rate * (decayed + MOMENTUM * moment_next)
    average_next = AVERAGE_KEEP * average + (1.0 - AVERAGE_KEEP) * weight_next
    return (weight_next, moment_next, average_next)


def local(
    tokens_in, cotangent, lengths, segments, bucket_map, bucket_tokens,
    attention, feedforward, vectors, head_bias, unit_bias,
    attention_moment, feedforward_moment, vectors_moment, head_moment, unit_moment,
    attention_mean, feedforward_mean, vectors_mean, head_mean, unit_mean,
):
    rows, width_d = tokens_in.shape
    layer_count = attention.shape[0]
    iy, ix, ic, ih, ib = (lax.axis_index(name) for name in EVERY)
    x_size = lax.axis_size("x")
    fast = lax.axis_size("y") == 2 and x_size == 2
    dp_size = lax.axis_size("y") * x_size * 2
    dp_place = (iy * x_size + ix) * 2 + ic
    mp_place = 2 * ih + ib
    quarter = 2 * ic + ib
    stays = ic == ih
    pack_length = rows * 4
    nb = pack_length // BLK

    low_attention, low_feedforward, low_vectors, low_head, low_unit = lax.optimization_barrier(
        tuple(p.astype(BF) for p in (attention, feedforward, vectors, head_bias, unit_bias))
    )
    head_width, units = attention.shape[3], feedforward.shape[3]
    qkv_low = jnp.concatenate([low_attention[:, i] for i in range(3)], axis=2)
    rows_w = attention.shape[2]
    spare_width = units // rows_w if fast else 0
    spare = jnp.zeros((layer_count, rows_w, PAD - head_width - spare_width), BF)
    if fast:
        spare = jnp.concatenate([low_unit.reshape(layer_count, rows_w, spare_width), spare], axis=2)
    ff_low = [
        jnp.concatenate([low_feedforward[layer, 0], low_feedforward[layer, 1],
                         low_attention[layer, 3], spare[layer]], axis=1)
        for layer in range(layer_count)
    ]

    hidden_low = home(tokens_in)
    meta = jnp.concatenate([segments[0], jnp.sum(lengths[0])[None], bucket_map])
    meta = jnp.where(stays, meta, swap(meta, "c"))
    segment_row, total_live, bucket = meta[:pack_length], meta[pack_length], meta[pack_length + 1]

    if fast:
        v8 = double(double(double(low_vectors.reshape(1, layer_count * 6, -1), "c"), "x"), "y")
        v8 = v8.reshape(2, 2, 2, layer_count * 6, -1)
        for axis, place in ((0, iy), (1, ix), (2, ic)):
            v8 = jnp.where(place == 1, jnp.flip(v8, axis), v8)
        full_vectors = v8.reshape(8, layer_count * 6, -1).transpose(1, 0, 2).reshape(layer_count, 6, width_d)
        head_pad = jnp.pad(low_head, ((0, 0), (0, 14), (0, 2 * head_width)))
        packed = jnp.concatenate([qkv_low, head_pad], axis=1)
        far = swap(packed, "h")
        mine, theirs = jnp.where(stays, packed, far), jnp.where(stays, far, packed)
        heads_used = mine[:, rows_w:rows_w + 2, :head_width]
        both_cores = jnp.stack([mine[:, :rows_w], swap(theirs[:, :rows_w], "c")])
        across = swap(both_cores, "x")
        qkv_parts = [both_cores, across, swap(both_cores, "y"), swap(across, "y")]
        chunk_places = [dp_place ^ (2 * (p % 4) + p // 4) for p in range(8)]
        turned = [2 * (i % 2) + i // 2 for i in range(4)]
        slots = jnp.stack([jnp.where(stays, turned[i], turned[i ^ 2]) for i in range(4)])
        specs = [(0, 0, 4), (1, 0, 4), (2, 0, 4), (3, 0, 2), (3, 2, 2)]
        specs = tuple(specs + [(chunk + 4, first, count) for chunk, first, count in specs])
        groups = ((0, 1, 2, 3), (7,), (4, 5, 6))
    else:
        full_vectors = lax.all_gather(low_vectors, ROWS_AXES, axis=2, tiled=True)
        units4 = lax.all_gather(low_unit, COLS_AXES, axis=0)
        heads_used = lax.all_gather(low_head, COLS_AXES, axis=0)[quarter]
        qkv_parts = [lax.all_gather(lax.all_gather(qkv_low, ROWS_AXES, axis=1, tiled=True), COLS_AXES, axis=0)[quarter][None]]
        whole_ff = [lax.all_gather(lax.all_gather(w, ROWS_AXES, axis=0, tiled=True), COLS_AXES, axis=0) for w in ff_low]
        chunk_places = [jnp.int32(0)]
        slots = jnp.stack([quarter ^ i for i in range(4)])
        specs = ((0, 0, 4),)
        groups = ((0,),)
    vec = f32(full_vectors)
    head_rows = f32(heads_used)

    positions = jnp.arange(pack_length, dtype=jnp.int32)
    own_segment = jnp.where(positions < total_live, segment_row, 64 + positions)
    by_block = own_segment.reshape(nb, BLK)
    first_block = jnp.sum(own_segment[None, :] < by_block[:, :1], axis=1) // BLK
    end_block = (jnp.sum(own_segment[None, :] <= by_block[:, -1:], axis=1) + BLK - 1) // BLK
    places = jnp.stack([quarter ^ rel for rel in range(4)])
    chunk_array = jnp.stack(chunk_places).astype(jnp.int32)
    scal = jnp.concatenate([first_block, end_block, places, jnp.zeros((1,), jnp.int32), chunk_array]).astype(jnp.int32)
    scal_rows = jnp.concatenate([slots.astype(jnp.int32), chunk_array])
    segk, segq = own_segment[:, None], own_segment[None, :]
    live_own = (quarter * rows + jnp.arange(rows) < total_live)[:, None]
    counts_float = f32(bucket_tokens)
    chosen = jnp.arange(bucket_tokens.shape[0]) == bucket
    pack_weight = bucket_tokens.shape[0] * jnp.sum(jnp.where(chosen, counts_float, 0.0)) / jnp.sum(counts_float)

    def vec_rows(layer, other):
        return jnp.concatenate([vec[layer], jnp.zeros((2, width_d), F32), vec[other], jnp.zeros((2, width_d), F32)])

    hidden = f32(hidden_low)
    normal, _ = normal_rows(hidden)
    normed = (normal * vec[0, 0] + vec[0, 1]).astype(BF)
    saved = []
    if fast:
        line = double(double(ff_low[0][None], "h"), "b")
        x_part, y_part = swap(line, "x"), swap(line, "y")
    for layer in range(layer_count):
        last = layer == layer_count - 1
        over = swap(normed, "b")
        normed_parts = [normed, over, swap(normed, "c"), swap(over, "c")]
        if fast:
            if layer:
                normed_parts, x_part, y_part = lax.optimization_barrier((normed_parts, x_part, y_part))
            if not last:
                ahead = after(ff_low[layer + 1][None], *normed_parts)
                ahead_h = swap(ahead, "h")
            own_parts = [line, x_part, y_part]
            if layer:
                own_parts += [swap(y_part[:2], "x"), swap(x_part[2:], "y")]
        mixed, log_total = attn_fwd(scal, normed_parts, qkv_parts, layer, head_rows[layer], segk, segq)
        if fast:
            if not last:
                mixed, ahead_h = lax.optimization_barrier((mixed, ahead_h))
            if layer:
                mixed, own_parts = lax.optimization_barrier((mixed, own_parts))
            else:
                mixed, x_part, y_part = lax.optimization_barrier((mixed, x_part, y_part))
                own_parts = [line, x_part, y_part, swap(y_part[:2], "x"), swap(x_part[2:], "y")]
        own_mixed = [mixed[0], swap(mixed[1], "b"), swap(mixed[2], "c"), corner(mixed[3])]
        vec16 = vec_rows(layer, 0 if last else layer + 1)
        if fast:
            at = 2 * units + head_width
            unit_row = f32(line[:, :, at:at + spare_width].reshape(4, 1, units))
            parts = own_parts + [swap(part, "c") for part in own_parts]
            if not last:
                ahead = jnp.concatenate([ahead, ahead_h])
                ahead_b = swap(after(ahead, *own_mixed), "b")
                own_mixed, ahead_b = lax.optimization_barrier((own_mixed, ahead_b))
                line = jnp.concatenate([ahead, ahead_b])
                x_part, y_part = swap(line, "x"), swap(line, "y")
        else:
            parts = [whole_ff[layer]]
            unit_row = f32(units4[:, layer][:, None, :])
        outs = post_fwd(scal_rows, own_mixed, hidden, vec16, unit_row, parts, specs, last)
        saved.append((hidden, normed_parts, mixed, log_total, own_mixed, outs[0], unit_row, vec16, parts))
        hidden = outs[1]
        if not last:
            normed = outs[2]
    hidden_out = f32(home(jnp.where(live_own, hidden, 0.0).astype(BF)))
    hidden_out = jnp.where(stays, jnp.where(live_own, hidden, 0.0), hidden_out)

    cotangent_here = home(after(cotangent, saved[0][5]))
    upstream = jnp.where(live_own, f32(cotangent_here) * pack_weight, 0.0)
    qkv_grads, matrix_grads, vector_grads, head_grads, unit_grads = [], [], [], [], []
    waiting = None
    for layer in reversed(range(layer_count)):
        hidden, normed_parts, mixed, log_total, own_mixed, middle, unit_row, vec16, parts = saved[layer]
        outs = post_bwd(scal_rows, own_mixed, middle, upstream, vec16, unit_row, parts, specs, groups)
        if waiting is not None:
            outs, beside = lax.optimization_barrier((outs, waiting[1:]))
            own = waiting[0]() + f32(beside[0]) + f32(beside[1])
        upstream, d_unit, d_vec = outs[:3]
        d_mixed, terms = outs[3:7], outs[7:]
        d_parts = [d_mixed[0], swap(d_mixed[1], "b"), swap(d_mixed[2], "c"), corner(d_mixed[3])]
        if fast:
            keep, send_far, send = terms
            far_sum = (f32(keep[3]) + f32(swap(send_far, "c")[0])).astype(BF)
            rest = swap(after(send, *d_parts), "c")
            for_x, for_y = swap(far_sum[2:], "y"), swap(far_sum[:2], "x")
            if waiting is not None:
                to_b = swap(after(own[2:].astype(BF), *d_parts), "b")
        outs = attn_bwd(scal, normed_parts, qkv_parts, layer, d_parts, mixed, head_rows[layer], segk, segq, log_total)
        if fast:
            outs, rest, for_x, for_y = lax.optimization_barrier((outs, rest, for_x, for_y))
            if waiting is not None:
                outs, to_b = lax.optimization_barrier((outs, to_b))
                above = own[:2] + f32(to_b)
            waiting = reduce_plane(keep, rest, for_x, for_y)
        else:
            matrix_grads.append(scatter(terms[0][0]))
        d_rows, d_head = outs[:2]
        qkv_grads.append(outs[2:])
        got = swap(d_rows[2:4], "c")
        got2 = swap((f32(d_rows[1]) + f32(got[1])).astype(BF), "b")
        if fast and not layer:
            got2, above_h = lax.optimization_barrier((got2, swap(above[1].astype(BF), "h")))
        d_normed = f32(d_rows[0]) + f32(got[0]) + f32(got2)
        normal, inverse = normal_rows(hidden)
        upstream = upstream + norm_back(d_normed, normal, inverse, vec[layer, 0])
        vector_grads.append(jnp.concatenate([
            jnp.sum(d_normed * normal, axis=0)[None], jnp.sum(d_normed, axis=0)[None], d_vec[2:6]]))
        head_grads.append(d_head)
        unit_grads.append(d_unit[:, 0])
    vector_sum = jnp.stack(vector_grads[::-1])
    head_sum = jnp.stack(head_grads[::-1])
    unit_sum = jnp.stack(unit_grads[::-1], axis=1)
    v_size, u_size = vector_sum.size, unit_sum.size // 4
    if fast:
        by_core = [jnp.stack([grads[core] for grads in qkv_grads[::-1]]) for core in range(2)]
        other = swap(by_core[1], "c")
        beside, other = lax.optimization_barrier((waiting[1:], other))
        own = waiting[0]() + f32(beside[0]) + f32(beside[1])
        to_hb, to_b = swap(own[3].astype(BF), "b"), swap(own[2].astype(BF), "b")
        to_hb, returned = lax.optimization_barrier((to_hb, home(upstream.astype(BF))))
        hop_h = (own[1] + f32(to_hb)).astype(BF)
        hop_h, vector_sum, other = lax.optimization_barrier((hop_h, vector_sum, other))
        to_h = swap(hop_h, "h")
        both = jnp.stack([jnp.where(stays, by_core[0], other), jnp.where(stays, other, by_core[0])])
        sides = swap(both[:, :, 1], "x"), swap(both[:, :, 2], "y"), diagonal(both[:, :, 3])
        flat_v, flat_e, flat_u = vector_sum.reshape(-1), head_sum.reshape(-1), unit_sum.reshape(4, -1)
        near_e = jnp.where(stays, flat_e, 0.0)
        got_h = swap(jnp.concatenate([flat_v, flat_u[1], flat_e - near_e]), "h")
        got_b = swap(jnp.concatenate([flat_v, flat_u[2]]), "b")
        got_hb = line_corner(jnp.concatenate([flat_v, flat_u[3]]))
        got_h, got_b, got_hb, to_h = lax.optimization_barrier((got_h, got_b, got_hb, to_h))
        flat = jnp.concatenate([flat_v, flat_u[0], near_e]) + got_h + jnp.pad(got_b + got_hb, (0, flat_e.size))
        others = swap(flat, "x"), swap(flat, "y"), diagonal(flat)
        both = f32(both[:, :, 0]) + f32(sides[0]) + f32(sides[1]) + f32(sides[2])
        qkv_gradient = both[0] + f32(swap(both[1].astype(BF), "h"))
        flat = flat + others[0] + others[1] + others[2]
        flat = flat + swap(flat, "c")
        vector_total = flat[:v_size].reshape(vector_sum.shape)
        unit_gradient = flat[v_size:v_size + u_size].reshape(unit_bias.shape)
        head_gradient = flat[v_size + u_size:].reshape(head_bias.shape)
        matrix_grads += [above[0] + f32(above_h), own[0] + f32(to_b) + f32(to_h)]
    else:
        empty = jnp.zeros((4,) + qkv_grads[0][0].shape[1:], F32)
        qkv_gradient = jnp.stack([scatter(empty.at[quarter].set(f32(grads[0][0]))) for grads in qkv_grads[::-1]])
    matrix_gradient = jnp.stack(matrix_grads[::-1])
    attention_gradient = jnp.stack(
        [qkv_gradient[:, :, i * head_width:(i + 1) * head_width] for i in range(3)]
        + [matrix_gradient[:, :, 2 * units:2 * units + head_width]], axis=1)
    feedforward_gradient = jnp.stack([matrix_gradient[:, :, :units], matrix_gradient[:, :, units:2 * units]], axis=1)

    if not fast:
        placed = jnp.zeros((4,) + head_sum.shape, F32).at[quarter].set(head_sum)
        vector_total, unit_total, head_total = lax.psum((vector_sum, unit_sum, placed), EVERY)
        unit_gradient, head_gradient = unit_total[mp_place], head_total[mp_place]
    chunk = width_d // dp_size
    vectors_gradient = lax.dynamic_slice_in_dim(vector_total, dp_place * chunk, chunk, 2)

    if not fast:
        returned = home(upstream.astype(BF))
    input_gradient = jnp.where(stays, upstream, f32(returned))
    step_rate = RATE_SCALE * lax.rsqrt(jnp.float32(dp_size * pack_length))
    weights = (attention, feedforward, vectors, head_bias, unit_bias)
    gradients = (attention_gradient, feedforward_gradient, vectors_gradient, head_gradient, unit_gradient)
    moments = (attention_moment, feedforward_moment, vectors_moment, head_moment, unit_moment)
    averages = (attention_mean, feedforward_mean, vectors_mean, head_mean, unit_mean)
    steps = [sgd_step(*leaf, step_rate) for leaf in zip(weights, gradients, moments, averages)]
    return (
        (hidden_out, input_gradient) + gradients + tuple(s[0] for s in steps) + tuple(s[1] for s in steps)
        + tuple(s[2] for s in steps) + (steps[0][0].astype(BF), steps[1][0].astype(BF))
    )


def solution(mesh):
    dp_size = mesh.shape["dp"]
    inner = jax.sharding.Mesh(mesh.devices.reshape(2, dp_size // 4, 2, 2, 2), EVERY)
    rows, cols = ROWS_AXES, COLS_AXES
    tokens = P(rows + cols, None)
    params = (P(None, None, rows, cols), P(None, None, rows, cols), P(None, None, rows), P(None, None, cols), P(None, cols))
    in_specs = (tokens, tokens, P(rows, None), P(rows, None), P(rows), P()) + params * 3
    out_specs = (tokens, tokens) + params * 4 + params[:2]
    return jax.shard_map(local, mesh=inner, in_specs=in_specs, out_specs=out_specs, check_vma=False)
```
